256 devices in a mesh: dp: 8 (over y, core), expert: 32 (over x, z).
Axes of the slice: x: 4, y: 4, z: 8, core: 2. Of those that a mesh axis runs over, the one named last changes fastest.
Arguments:
- cotangent: bfloat16 [32768, 2048], P(('dp', 'expert')), may hold values from -6 to 6
- gate_prob: bfloat16 [32768, 8], P(('dp', 'expert')), may hold values from 0.029907227 to 0.3984375
- routes: int32 [32768, 8], P(('dp', 'expert')), may hold values from 0 to 63, all different within a row; in each aligned block of 128 rows (0 to 127, 128 to 255, ...) at most 24 rows name the same one
- hidden: bfloat16 [8, 64, 32, 24, 768], P('dp', 'expert'), may hold values from -0.3984375 to 0.3984375
- down_weight: bfloat16 [64, 768, 2048], P('expert'), may hold values from -0.21875 to 0.21875
- sign_seed: int32 [2048], replicated, may hold values from 0 to 1
Outputs:
- grad_hidden: bfloat16 [8, 64, 32, 24, 768], P('dp', 'expert')
- grad_prob: float32 [32768, 8], P(('dp', 'expert'))
- grad_weight: float32 [2048, 64, 768], P('dp', 'expert')
The draws below stay inside these ranges and needn't reach their ends.
Inputs may be any that keep to these rules, and one draw needn't show every extreme that they name: `routes`: each row names 8 different experts; in each device's block of 128 tokens no expert is named by more than 24 tokens, and in some block one expert is named by exactly 24.
All inputs are finite; a program needn't handle non-finite values.
Results may differ from the reference program's by a relative error of at most 0.015.
Values may be sent and summed in bfloat16 or wider, within the bound.
A program may use at most 128 MiB of HBM per device.

```python
import math
import jax
import jax.numpy as jnp
import numpy as np
from jax import lax

D = 2048
FF = 768
TOPK = 8
BLOCK = 128
TOK_DEV = 128
GROUPS = 8
SOURCES = 32
EXPERTS = 64
TOKENS = 32768
CAP = 24


def touch_ends(array, stream_key, least, largest):
    shape = array.shape
    index_at = [jax.random.randint(jax.random.fold_in(stream_key, axis), (), 0, shape[axis]) for axis in range(len(shape))]
    array = array.at[tuple(index_at)].set(least)
    longest = shape.index(max(shape))
    index_at[longest] = (index_at[longest] + 1) % shape[longest]
    return array.at[tuple(index_at)].set(largest)


def steps_of(stream_key, shape, shards, smallest, largest):
    level, own = 1.0, jax.random.fold_in(stream_key, 6)
    for axis_at, blocks in shards:
        draws = jnp.exp(jax.random.uniform(jax.random.fold_in(own, axis_at), (blocks,), jnp.float32, smallest / len(shards), largest / len(shards)))
        level = level * jnp.repeat(draws, shape[axis_at] // blocks).reshape([-1 if axis == axis_at else 1 for axis in range(len(shape))])
    return level


def routed_block(own_key, own, number, rows, count, top, most, skew):
    order = jax.random.permutation(own_key, count)
    crowded, ordinary = portions_of(count, rows * top, most, skew, True), portions_of(count, rows * top, most, skew, False)
    places = jnp.arange(count)

    def named(tallies, turn):
        used = int((tallies > 0).sum())
        fixed = max(1, used // 4)
        passed = fixed + (places - fixed + turn * (used - fixed)) % max(1, count - fixed)
        return jnp.zeros((count,), jnp.int32).at[order[jnp.where(places < fixed, places, passed)]].set(jnp.asarray(tallies, jnp.int32))

    tallies = jnp.where(number % 4 == 0, named(crowded, number // 4), named(ordinary, number - number // 4 - 1))
    mixed = jax.random.permutation(jax.random.fold_in(own, 3), count)
    source_of, taker = mixed[0:count // 2 * 2:2], mixed[1:count // 2 * 2:2]
    room = jnp.minimum(tallies[source_of] - 1, most - tallies[taker]) // 2
    room = jnp.where((source_of == order[0]) | (taker == order[0]) | (tallies[taker] == 0), 0, jnp.maximum(room, 0))
    passed = jax.random.randint(jax.random.fold_in(own, 4), (count // 2,), 0, 1 << 20) % (room + 1)
    tallies = tallies.at[source_of].add(-passed).at[taker].add(passed)
    labels = jnp.searchsorted(jnp.cumsum(tallies), jnp.arange(rows * top), side="right").astype(jnp.int32)
    grid = labels.reshape(top, rows).T
    grid = grid[jax.random.permutation(jax.random.fold_in(own, 1), rows)]
    turn = jax.random.randint(jax.random.fold_in(own, 2), (rows, 1), 0, top)
    return jnp.take_along_axis(grid, (jnp.arange(top)[None, :] + turn) % top, axis=1)


def portions_of(count, total, limit, lean, full):
    loads = [(1 << 20) // math.isqrt(standing ** lean) + 1 for standing in range(1, count + 1)]
    largest = limit if full else min(limit, max(-(-total // count), total * loads[0] // sum(loads)))
    least = 1 if total - largest >= count - 1 else 0
    given, spare = [largest] + [least] * (count - 1), total - largest - least * (count - 1)
    while spare > 0:
        free = [i for i in range(1, count) if given[i] < largest] or [i for i in range(1, count) if given[i] < limit]
        mass, left = sum([loads[i] for i in free]), spare
        for i in free:
            extra = min(limit - given[i], max(1, left * loads[i] // mass), spare)
            given[i] = given[i] + extra
            spare = spare - extra
    return np.array(given)


def normal_values(key, shape, scale, limit, cuts=(), kind=jnp.bfloat16):
    array = scale * jax.random.normal(key, shape, jnp.float32)
    if cuts:
        array = array * steps_of(key, shape, cuts, -0.22, 0.18)
    return jnp.clip(array, -limit, limit).astype(kind)


def setup_inputs(seed: int = 0) -> dict:
    arg_keys = jax.random.split(jax.random.key(seed), 7)
    cotangent = normal_values(arg_keys[0], (TOKENS, D), 1.0, 6.0, ((0, 256),))
    gate_prob = jnp.clip(jnp.exp(math.log(0.3984375) - 2.5894505 * jax.random.uniform(arg_keys[1], (TOKENS, TOPK), jnp.float32) ** steps_of(arg_keys[1], (TOKENS, TOPK), ((0, 256),), -0.2, 0.2)), 0.029907227, 0.3984375).astype(jnp.bfloat16)
    routes_keys = jax.random.split(jax.random.fold_in(arg_keys[2], 1), TOKENS // TOK_DEV)
    routes_turns = jax.random.permutation(jax.random.fold_in(arg_keys[2], 3), TOKENS // TOK_DEV)
    routes = jax.vmap(lambda own, number: routed_block(jax.random.fold_in(arg_keys[2], 2), own, number, TOK_DEV, EXPERTS, TOPK, CAP, 2))(routes_keys, routes_turns).reshape((TOKENS, TOPK))
    hidden = normal_values(arg_keys[3], (GROUPS, EXPERTS, SOURCES, CAP, FF), 0.05, 0.3984375, ((0, 8), (1, 32)))
    down_weight = normal_values(arg_keys[4], (EXPERTS, FF, D), FF ** -0.5, 0.21875, ((0, 32),))
    sign_seed = touch_ends(jax.random.randint(arg_keys[5], (D,), 0, 2), jax.random.fold_in(arg_keys[5], 1), 0, 1).astype(jnp.int32)
    return {"cotangent": cotangent, "gate_prob": gate_prob, "routes": routes, "hidden": hidden, "down_weight": down_weight, "sign_seed": sign_seed}


def hadamard(length):
    index_vec = jnp.arange(length, dtype=jnp.int32)
    anded = jnp.bitwise_and(index_vec[:, None], index_vec[None, :])
    parity = jnp.zeros((length, length), jnp.int32)
    for shift_by in range(max(length.bit_length() - 1, 1)):
        parity = parity + jnp.bitwise_and(jnp.right_shift(anded, shift_by), 1)
    return (1.0 - 2.0 * (parity % 2).astype(jnp.float32)) / math.sqrt(length)

def block_slots(routes, experts_all):
    hit_count = lax.optimization_barrier(jnp.sum((routes[:, :, None] == jnp.arange(experts_all, dtype=jnp.int32)).astype(jnp.int32), axis=1, dtype=jnp.int32))
    before = jnp.cumsum(hit_count, axis=0, dtype=jnp.int32) - hit_count
    return jnp.take_along_axis(before, routes, axis=1)

def reference(cotangent, gate_prob, routes, hidden, down_weight, sign_seed):
    block_total = GROUPS * SOURCES
    blocks = routes.reshape(block_total, TOK_DEV, TOPK)
    slot_rank = jax.vmap(block_slots, in_axes=(0, None))(blocks, EXPERTS)
    block_id = jnp.arange(block_total, dtype=jnp.int32)[:, None, None]
    group = block_id // SOURCES
    source = block_id % SOURCES
    position = ((blocks * GROUPS + group) * SOURCES + source) * CAP + slot_rank
    pair_count = TOKENS * TOPK
    pair_table = jnp.full((EXPERTS * GROUPS * SOURCES * CAP,), pair_count, jnp.int32)
    pair_table = pair_table.at[position.reshape(-1)].set(jnp.arange(pair_count, dtype=jnp.int32))
    pair_table = pair_table.reshape(EXPERTS, GROUPS, SOURCES, CAP)
    sign_vec = (2 * sign_seed - 1).astype(jnp.float32)
    rotation = hadamard(BLOCK)
    flat_gate = gate_prob.reshape(-1)

    def per_expert(expert):
        slot_table = lax.dynamic_index_in_dim(pair_table, expert, 0, keepdims=False).reshape(-1)
        routed_rows = jnp.take(cotangent, slot_table // TOPK, axis=0, mode='fill', fill_value=0)
        weights_here = jnp.take(flat_gate, slot_table, axis=0, mode='fill', fill_value=0).astype(jnp.float32)[:, None]
        saved_rows = lax.dynamic_index_in_dim(hidden, expert, 1, keepdims=False).reshape(-1, FF)
        weight = lax.dynamic_index_in_dim(down_weight, expert, 0, keepdims=False)
        back_grad = jnp.dot(routed_rows, weight.T, preferred_element_type=jnp.float32)
        hidden_grad = (weights_here * back_grad).astype(jnp.bfloat16)
        slot_grad = lax.optimization_barrier(jnp.sum(back_grad * saved_rows.astype(jnp.float32), axis=1))
        weighted = (weights_here * saved_rows.astype(jnp.float32)).astype(jnp.bfloat16)
        per_group = jnp.einsum('gxd,gxf->gdf', routed_rows.reshape(GROUPS, -1, D).astype(jnp.float32), weighted.reshape(GROUPS, -1, FF).astype(jnp.float32))
        shaped = per_group.reshape(GROUPS, D // BLOCK, BLOCK, FF) * sign_vec.reshape(1, D // BLOCK, BLOCK, 1)
        turned = jnp.einsum('ij,gbjf->gbif', rotation, shaped, precision=lax.Precision.HIGHEST)
        rounded = lax.optimization_barrier(turned.astype(jnp.bfloat16)).astype(jnp.float32)
        summed = lax.optimization_barrier(jnp.sum(rounded, axis=0)).reshape(D, FF)
        return (hidden_grad.reshape(GROUPS, SOURCES, CAP, FF), slot_grad, summed)
    hidden_grad, slot_grad, summed = lax.map(per_expert, jnp.arange(EXPERTS, dtype=jnp.int32))
    grad_hidden = jnp.transpose(hidden_grad, (1, 0, 2, 3, 4))
    grad_prob = slot_grad.reshape(-1)[position.reshape(-1)].reshape(TOKENS, TOPK)
    grad_weight = jnp.transpose(summed, (1, 0, 2))
    return (grad_hidden, grad_prob, grad_weight)
```

```python
import functools
import math

import jax
import jax.numpy as jnp
from jax import lax
from jax.experimental import pallas as pl
from jax.experimental.pallas import tpu as pltpu
from jax.sharding import PartitionSpec as P

MESH = pl.DeviceIdType.MESH
BLOCK = 128
NX, NY, NZ = 4, 4, 8
CH = 4
LANES = 128
CW = NY * LANES
MISS = -100.0
BF16, F32 = jnp.bfloat16, jnp.float32


def dot_nn(a, b):
    return lax.dot_general(a, b, (((1,), (0,)), ((), ())), preferred_element_type=F32)


def dot_nt(a, b):
    return lax.dot_general(a, b, (((1,), (1,)), ((), ())), preferred_element_type=F32)


def kernel(
    cot, hid_hbm, w_hbm, routes_t, gate_t, seed,
    gh_out, gp_out, gw_out,
    zbuf, sel, rg, xsend, relay_r, relay_l, wbuf, hid, weighted_t, acc,
    part, part_in, y_relay, y_fin, tab, gtab, s_tab, z_tab, d_tab, r_tab, r_mid, r_end,
    in_sem, w_sem, hid_sem,
    zs_full, zs_half, z_recv,
    xs_sem, x_recv, xrel_recv,
    tz_send, tz_recv, tx_send, tx_recv,
    p_send, p_recv, yr_send, yr_recv, yf_send, yf_recv,
    rx_send, rx_recv, rz_send, rz_recv,
):
    rows48 = 48
    dp = lax.axis_index("dp")
    ex = lax.axis_index("expert")
    y, core = dp // 2, lax.rem(dp, 2)
    x, z = ex // NZ, lax.rem(ex, NZ)
    up = lambda v, d, n: lax.rem(v + d, n)

    def x_dev(xx):
        return (dp, xx * NZ + z)

    def z_dev(zz):
        return (dp, x * NZ + zz)

    xr, xl = x_dev(up(x, 1, NX)), x_dev(up(x, NX - 1, NX))
    zr, zl = z_dev(up(z, 1, NZ)), z_dev(up(z, NZ - 1, NZ))
    yr, yl = (up(y, 1, NY) * 2 + core, ex), (up(y, NY - 1, NY) * 2 + core, ex)
    partner = (y * 2 + 1 - core, ex)

    def remote(src, dst, send, recv, dev):
        return pltpu.make_async_remote_copy(
            src_ref=src, dst_ref=dst, send_sem=send, recv_sem=recv,
            device_id=dev, device_id_type=MESH,
        )

    def wait_recv(dst, sem):
        remote(dst, dst, sem, sem, xr).wait_recv()

    def wait_send(src, sem):
        remote(src, src, sem, sem, xr).wait_send()

    for c in range(CH):
        for yy in range(NY):
            base = 512 * yy + 256 * (c % 2) + 128 * (c // 2)
            pltpu.make_async_copy(
                cot.at[:, pl.ds(base, LANES)],
                zbuf.at[c, z, :, pl.ds(LANES * yy, LANES)], in_sem.at[c],
            ).start()
    pltpu.make_async_copy(hid_hbm, hid, hid_sem).start()
    for c in range(CH):
        for yy in range(NY):
            base = 512 * yy + 256 * (c % 2) + 128 * (c // 2)
            pltpu.make_async_copy(
                w_hbm.at[:, :, pl.ds(base, LANES)],
                wbuf.at[c, :, :, pl.ds(LANES * yy, LANES)], w_sem.at[c],
            ).start()

    e_iota = lax.broadcasted_iota(jnp.int32, (64, LANES), 0)
    hit = jnp.zeros((64, LANES), F32)
    gate = jnp.zeros((64, LANES), F32)
    for k in range(8):
        eq = routes_t[k:k + 1, :] == e_iota
        hit = jnp.where(eq, 1.0, hit)
        gate = jnp.where(eq, gate_t[k:k + 1, :], gate)
    earlier = (
        lax.broadcasted_iota(jnp.int32, (LANES, LANES), 0)
        < lax.broadcasted_iota(jnp.int32, (LANES, LANES), 1)
    )
    rank = dot_nn(hit.astype(BF16), jnp.where(earlier, 1.0, 0.0).astype(BF16))
    tab[...] = jnp.where(hit > 0.5, rank, MISS)
    gtab[...] = gate
    for zz in range(NZ):
        for xx in range(NX):
            e = 16 * xx + 2 * zz
            s_tab[zz, xx, 0:2, :] = tab[e:e + 2, :]
            s_tab[zz, xx, 2:4, :] = gtab[e:e + 2, :]
            s_tab[zz, xx, 4:8, :] = jnp.zeros((4, LANES), F32)

    barrier = pltpu.get_barrier_semaphore()
    peers = [z_dev(up(z, d, NZ)) for d in range(1, NZ)]
    peers += [x_dev(up(x, d, NX)) for d in range(1, NX)]
    peers += [yr, yl, partner]
    for peer in peers:
        pl.semaphore_signal(barrier, inc=1, device_id=peer, device_id_type=MESH)
    pl.semaphore_wait(barrier, len(peers))

    for d in range(1, NZ):
        to = up(z, d, NZ)
        remote(s_tab.at[to], z_tab.at[z], tz_send.at[d], tz_recv.at[d], z_dev(to)).start()
    z_tab[z] = s_tab[z]

    def z_send(c, h):
        right, left = up(z, NZ - h, NZ), up(z, h, NZ)
        if h < 3:
            remote(zbuf.at[c, right], zbuf.at[c, right], zs_full.at[c, 0], z_recv.at[c, 0, h], zr).start()
            remote(zbuf.at[c, left], zbuf.at[c, left], zs_full.at[c, 1], z_recv.at[c, 1, h], zl).start()
        else:
            a, b = pl.ds(0, 64), pl.ds(64, 64)
            remote(zbuf.at[c, right, a], zbuf.at[c, right, a], zs_half.at[c, 0], z_recv.at[c, 0, h], zr).start()
            remote(zbuf.at[c, left, b], zbuf.at[c, left, b], zs_half.at[c, 1], z_recv.at[c, 1, h], zl).start()

    def z_wait(c, dist):
        from_left, from_right = up(z, NZ - dist, NZ), up(z, dist, NZ)
        if dist < 4:
            wait_recv(zbuf.at[c, from_left], z_recv.at[c, 0, dist - 1])
            wait_recv(zbuf.at[c, from_right], z_recv.at[c, 1, dist - 1])
        else:
            wait_recv(zbuf.at[c, from_left, pl.ds(0, 64)], z_recv.at[c, 0, dist - 1])
            wait_recv(zbuf.at[c, from_right, pl.ds(64, 64)], z_recv.at[c, 1, dist - 1])

    def in_wait(c):
        pltpu.make_async_copy(zbuf.at[c, z], zbuf.at[c, z], in_sem.at[c]).wait()

    in_wait(0)
    z_send(0, 0)

    for d in range(1, NZ):
        wait_recv(z_tab.at[up(z, NZ - d, NZ)], tz_recv.at[d])
    r_iota = lax.broadcasted_iota(jnp.int32, (rows48, LANES), 0).astype(F32)

    def one_hot_pair(even_row, odd_row):
        return even_row == r_iota, odd_row + 24.0 == r_iota

    def build_sel(m, _):
        for dx in range(NX):
            xx = up(x, dx, NX)
            for j in range(2):
                even, odd = one_hot_pair(
                    z_tab[2 * m, xx, j:j + 1, :], z_tab[2 * m + 1, xx, j:j + 1, :]
                )
                at = (dx * 2 + j) * rows48
                sel[m, at:at + rows48, 0:LANES] = jnp.where(even, 1.0, 0.0).astype(BF16)
                sel[m, at:at + rows48, LANES:2 * LANES] = jnp.where(odd, 1.0, 0.0).astype(BF16)
        return 0

    lax.fori_loop(0, 4, build_sel, 0)

    for d in range(1, NX):
        to = up(x, d, NX)
        remote(z_tab.at[:, to], d_tab.at[x], tx_send.at[d], tx_recv.at[d], x_dev(to)).start()
    d_tab[x] = z_tab[:, x]

    step_sign = 2 * lax.rem(z, 2) - 1
    pair_of = [up(z // 2, o, 4) for o in (0, 4 + step_sign, 4 - step_sign, 2)]

    def x_step(c, i):
        m = pair_of[i]
        tokens = zbuf[c, pl.ds(2 * m, 2)].reshape(2 * LANES, CW)
        rows = dot_nn(sel[m], tokens).astype(BF16)
        xsend[c, i] = rows[96:384].reshape(3, 2, rows48, CW)
        here = x * 4 + m
        remote(xsend.at[c, i, 1, 0], relay_r.at[c, i], xs_sem.at[c, 2], xrel_recv.at[c, i, 0], xr).start()
        remote(xsend.at[c, i, 1, 1], relay_l.at[c, i], xs_sem.at[c, 3], xrel_recv.at[c, i, 1], xl).start()
        remote(xsend.at[c, i, 0], rg.at[c, :, here], xs_sem.at[c, 0], x_recv.at[c, 0], xr).start()
        remote(xsend.at[c, i, 2], rg.at[c, :, here], xs_sem.at[c, 1], x_recv.at[c, 1], xl).start()
        rg[c, :, here] = rows[0:96].reshape(2, rows48, CW)

    def x_forward(c, i):
        m = pair_of[i]
        from_l, from_r = up(x, NX - 1, NX) * 4 + m, up(x, 1, NX) * 4 + m
        wait_recv(relay_r.at[c, i], xrel_recv.at[c, i, 0])
        remote(relay_r.at[c, i], rg.at[c, 0, from_l], xs_sem.at[c, 4], x_recv.at[c, 2], xr).start()
        wait_recv(relay_l.at[c, i], xrel_recv.at[c, i, 1])
        remote(relay_l.at[c, i], rg.at[c, 1, from_r], xs_sem.at[c, 5], x_recv.at[c, 3], xl).start()

    def x_wait(c):
        left, right, far = (pl.ds(up(x, d, NX) * 4, 4) for d in (3, 1, 2))
        wait_recv(rg.at[c, :, left], x_recv.at[c, 0])
        wait_recv(rg.at[c, :, right], x_recv.at[c, 1])
        wait_recv(rg.at[c, 0, far], x_recv.at[c, 2])
        wait_recv(rg.at[c, 1, far], x_recv.at[c, 3])

    def pair_rows(p, j, row):
        xs, zs = p // 4, 2 * lax.rem(p, 4)
        return d_tab[xs, zs, row + j:row + j + 1, :], d_tab[xs, zs + 1, row + j:row + j + 1, :]

    def slot_prob(p, j):
        even, odd = one_hot_pair(*pair_rows(p, j, 0))
        g_even, g_odd = pair_rows(p, j, 2)
        picked = jnp.where(even, g_even, 0.0) + jnp.where(odd, g_odd, 0.0)
        return jnp.sum(picked, axis=1, keepdims=True)

    def weigh():
        for d in range(1, NX):
            wait_recv(d_tab.at[up(x, NX - d, NX)], tx_recv.at[d])
        pltpu.make_async_copy(hid_hbm, hid, hid_sem).wait()

        def body(p, _):
            at = pl.ds(pl.multiple_of(p * rows48, 16), rows48)
            for j in range(2):
                rows = slot_prob(p, j) * hid[j, at, :].astype(F32)
                gh_out[j, at, :] = rows.astype(BF16)
            return 0

        lax.fori_loop(0, 16, body, 0)
        for j in range(2):
            for q in range(6):
                cols = slice(LANES * q, LANES * (q + 1))
                weighted_t[j, cols, :] = gh_out[j, :, cols].T

    def partial(c, j):
        for q in range(3):
            fs = slice(256 * q, 256 * (q + 1))
            got = dot_nn(weighted_t[j, fs, :], rg[c, j].reshape(768, CW)).astype(BF16)
            for yy in range(NY):
                part[c, yy, j, fs, :] = got[:, LANES * yy:LANES * (yy + 1)]

        @pl.when(lax.rem(c, 2) != core)
        def _():
            half = c // 2
            remote(part.at[c, :, j], part_in.at[half, :, j], p_send.at[half, j], p_recv.at[half, j], partner).start()

    def back(c, j):
        for q in range(3):
            rs = slice(256 * q, 256 * (q + 1))
            lhs = rg[c, j].reshape(768, CW)[rs]
            got = dot_nt(lhs, wbuf[c, j])

            acc[j, rs, :] += got

    def w_wait(c):
        pltpu.make_async_copy(wbuf.at[c], wbuf.at[c], w_sem.at[c]).wait()

    def pair_add(c, j):
        half = c // 2
        wait_recv(part_in.at[half, :, j], p_recv.at[half, j])

        def body(yy, _):
            total = part[c, yy, j].astype(F32) + part_in[half, yy, j].astype(F32)
            part[c, yy, j] = total.astype(BF16)
            return 0

        far = up(y, 2, NY)
        lax.fori_loop(0, NY, lambda o, t: body(up(far, o, NY), t), 0)
        if j == 0:
            remote(part.at[c, far, 0], y_relay.at[half, 0], yr_send.at[half, 0], yr_recv.at[half, 0], yr).start()
            near = up(y, 3, NY)
            remote(part.at[c, near, 0], y_fin.at[half, 1, 0], yf_send.at[half, 1, 0], yf_recv.at[half, 1, 0], yl).start()
        else:
            remote(part.at[c, far, 1], y_relay.at[half, 1], yr_send.at[half, 1], yr_recv.at[half, 1], yl).start()
            near = up(y, 1, NY)
            remote(part.at[c, near, 1], y_fin.at[half, 0, 1], yf_send.at[half, 0, 1], yf_recv.at[half, 0, 1], yr).start()

    def relay_add(c):
        half = c // 2
        for j, d, side, dev in ((0, 1, 0, yr), (1, 3, 1, yl)):
            near = up(y, d, NY)
            wait_recv(y_relay.at[half, j], yr_recv.at[half, j])
            total = part[c, near, j].astype(F32) + y_relay[half, j].astype(F32)
            part[c, near, j] = total.astype(BF16)
            remote(part.at[c, near, j], y_fin.at[half, side, j], yf_send.at[half, side, j], yf_recv.at[half, side, j], dev).start()

    def finish(c):
        half = c // 2
        i0 = lax.broadcasted_iota(jnp.int32, (BLOCK, BLOCK), 0)
        i1 = lax.broadcasted_iota(jnp.int32, (BLOCK, BLOCK), 1)
        bits = i0 & i1
        bits = bits ^ (bits >> 4)
        bits = bits ^ (bits >> 2)
        bits = bits ^ (bits >> 1)
        sign = (2 * seed[pl.ds(4 * y + 2 * core + half, 1), :] - 1).astype(F32)
        turn = (jnp.where((bits & 1) == 1, -1.0, 1.0) * sign).astype(BF16)
        out_rows = pl.ds(pl.multiple_of(half * BLOCK, BLOCK), BLOCK)
        for j in range(2):
            wait_recv(y_fin.at[half, 0, j], yf_recv.at[half, 0, j])
            wait_recv(y_fin.at[half, 1, j], yf_recv.at[half, 1, j])
            total = part[c, y, j].astype(F32) + y_fin[half, 0, j].astype(F32) + y_fin[half, 1, j].astype(F32)
            high = total.astype(BF16)
            low = (total - high.astype(F32)).astype(BF16)
            turned = (dot_nt(turn, high) + dot_nt(turn, low)) * (1.0 / math.sqrt(BLOCK))
            gw_out[out_rows, 768 * j:768 * (j + 1)] = turned

    acc[...] = jnp.zeros(acc.shape, F32)

    def chunk(c, _):
        owner = lambda v: lax.rem(v, 2) == core

        for i in range(4):
            @pl.when(c == 0)
            def _(i=i):
                z_wait(0, i + 1)
                if i < 3:
                    z_send(0, i + 1)

            if i == 3:
                @pl.when(c > 0)
                def _():
                    z_wait(c, 4)

            x_step(c, i)

            @pl.when(c + 1 < CH)
            def _(i=i):
                if i == 0:
                    in_wait(c + 1)
                else:
                    z_wait(c + 1, i)
                z_send(c + 1, i)

            if i == 0:
                @pl.when(c == 0)
                def _():
                    weigh()

                @pl.when(c > 0)
                def _():
                    x_forward(c - 1, 3)

                @pl.when((c > 1) & owner(c - 2))
                def _():
                    relay_add(c - 2)
            else:
                x_forward(c, i - 1)

            if i == 1:
                @pl.when(c > 0)
                def _():
                    x_wait(c - 1)
                    partial(c - 1, 0)

                @pl.when((c > 1) & owner(c - 2))
                def _():
                    finish(c - 2)
            if i == 2:
                @pl.when(c > 0)
                def _():
                    partial(c - 1, 1)
                    w_wait(c - 1)
                    back(c - 1, 0)
            if i == 3:
                @pl.when((c > 0) & owner(c - 1))
                def _():
                    pair_add(c - 1, 0)
                    pair_add(c - 1, 1)

                @pl.when(c > 0)
                def _():
                    back(c - 1, 1)
        return 0

    lax.fori_loop(0, CH, chunk, 0)

    last = CH - 1
    mine = core == last % 2
    x_forward(last, 3)

    @pl.when(core == (last - 1) % 2)
    def _():
        relay_add(last - 1)

    w_wait(last)
    x_wait(last)
    partial(last, 0)
    partial(last, 1)

    @pl.when(mine)
    def _():
        pair_add(last, 0)
        pair_add(last, 1)

    back(last, 0)

    @pl.when(core == (last - 1) % 2)
    def _():
        finish(last - 1)

    @pl.when(mine)
    def _():
        relay_add(last)

    back(last, 1)

    def outputs(p, _):
        at = pl.ds(pl.multiple_of(p * rows48, 16), rows48)
        xs, zs = p // 4, 2 * lax.rem(p, 4)
        for j in range(2):
            rows = acc[j, at, :]
            gh_out[j, at, :] = (slot_prob(p, j) * rows).astype(BF16)
            slot = jnp.sum(rows * hid[j, at, :].astype(F32), axis=1, keepdims=True)
            even, odd = one_hot_pair(*pair_rows(p, j, 0))
            r_tab[xs, zs, j:j + 1, :] = jnp.sum(jnp.where(even, slot, 0.0), axis=0, keepdims=True)
            r_tab[xs, zs + 1, j:j + 1, :] = jnp.sum(jnp.where(odd, slot, 0.0), axis=0, keepdims=True)
        return 0

    r_tab[...] = jnp.zeros(r_tab.shape, F32)
    lax.fori_loop(0, 16, outputs, 0)

    for d in range(1, NX):
        to = up(x, d, NX)
        remote(r_tab.at[to], r_mid.at[x], rx_send.at[d], rx_recv.at[d], x_dev(to)).start()
    r_mid[x] = r_tab[x]
    for d in range(1, NX):
        wait_recv(r_mid.at[up(x, NX - d, NX)], rx_recv.at[d])
    for d in range(1, NZ):
        to = up(z, d, NZ)
        remote(r_mid.at[:, to], r_end.at[z], rz_send.at[d], rz_recv.at[d], z_dev(to)).start()
    r_end[z] = r_mid[:, z]

    @pl.when(mine)
    def _():
        finish(last)

    for d in range(1, NZ):
        wait_recv(r_end.at[up(z, NZ - d, NZ)], rz_recv.at[d])
    grad_prob = jnp.zeros((8, LANES), F32)
    chosen = routes_t[...]
    for zz in range(NZ):
        for xx in range(NX):
            for j in range(2):
                e = 16 * xx + 2 * zz + j
                grad_prob = jnp.where(chosen == e, r_end[zz, xx, j:j + 1, :], grad_prob)
    gp_out[...] = grad_prob

    for d in range(1, NZ):
        wait_send(s_tab.at[0], tz_send.at[d])
        wait_send(r_mid.at[:, 0], rz_send.at[d])
    for d in range(1, NX):
        wait_send(z_tab.at[:, 0], tx_send.at[d])
        wait_send(r_tab.at[0], rx_send.at[d])
    for c in range(CH):
        for side in range(2):
            wait_send(zbuf.at[c, pl.ds(0, 3)], zs_full.at[c, side])
            wait_send(zbuf.at[c, 0, pl.ds(0, 64)], zs_half.at[c, side])
            wait_send(xsend.at[c, :, 2 * side], xs_sem.at[c, side])
            wait_send(xsend.at[c, :, 1, side], xs_sem.at[c, 2 + side])
            wait_send(relay_r.at[c], xs_sem.at[c, 4 + side])
        half = c // 2

        @pl.when(core == c % 2)
        def _(c=c, half=half):
            for j in range(2):
                wait_send(part.at[c, 0, 0], yr_send.at[half, j])
                for side in range(2):
                    wait_send(part.at[c, 0, 0], yf_send.at[half, side, j])

        @pl.when(core != c % 2)
        def _(c=c, half=half):
            for j in range(2):
                wait_send(part.at[c, :, j], p_send.at[half, j])


def shards(cotangent, gate_prob, routes, hidden, down_weight, sign_seed):
    tok, features = cotangent.shape
    _, pair, sources, cap, units = hidden.shape
    slots = sources * cap
    vm = pl.BlockSpec(memory_space=pltpu.VMEM)
    anyspec = pl.BlockSpec(memory_space=pl.ANY)
    dma = pltpu.SemaphoreType.DMA
    scratch = [
        pltpu.VMEM((CH, NZ, tok, CW), BF16),
        pltpu.VMEM((4, 384, 256), BF16),
        pltpu.VMEM((CH, 2, 16, 48, CW), BF16),
        pltpu.VMEM((CH, 4, 3, 2, 48, CW), BF16),
        pltpu.VMEM((CH, 4, 48, CW), BF16),
        pltpu.VMEM((CH, 4, 48, CW), BF16),
        pltpu.VMEM((CH, 2, units, CW), BF16),
        pltpu.VMEM((2, slots, units), BF16),
        pltpu.VMEM((2, units, slots), BF16),
        pltpu.VMEM((2, slots, units), F32),
        pltpu.VMEM((CH, NY, 2, units, LANES), BF16),
        pltpu.VMEM((2, NY, 2, units, LANES), BF16),
        pltpu.VMEM((2, 2, units, LANES), BF16),
        pltpu.VMEM((2, 2, 2, units, LANES), BF16),
        pltpu.VMEM((64, LANES), F32),
        pltpu.VMEM((64, LANES), F32),
        pltpu.VMEM((NZ, NX, 8, LANES), F32),
        pltpu.VMEM((NZ, NX, 8, LANES), F32),
        pltpu.VMEM((NX, NZ, 8, LANES), F32),
        pltpu.VMEM((NX, NZ, 8, LANES), F32),
        pltpu.VMEM((NX, NZ, 8, LANES), F32),
        pltpu.VMEM((NZ, NX, 8, LANES), F32),
        dma((CH,)), dma((CH,)), dma,
        dma((CH, 2)), dma((CH, 2)), dma((CH, 2, 4)),
        dma((CH, 6)), dma((CH, 4)), dma((CH, 4, 2)),
        dma((NZ,)), dma((NZ,)), dma((NX,)), dma((NX,)),
        dma((2, 2)), dma((2, 2)),
        dma((2, 2)), dma((2, 2)), dma((2, 2, 2)), dma((2, 2, 2)),
        dma((NX,)), dma((NX,)), dma((NZ,)), dma((NZ,)),
    ]
    grad_hidden, grad_prob, grad_weight = pl.pallas_call(
        kernel,
        out_shape=(
            jax.ShapeDtypeStruct((pair, slots, units), BF16),
            jax.ShapeDtypeStruct((8, tok), F32),
            jax.ShapeDtypeStruct((256, pair * units), F32),
        ),
        in_specs=[anyspec, anyspec, anyspec, vm, vm, vm],
        out_specs=(vm, vm, vm),
        scratch_shapes=scratch,
        compiler_params=pltpu.CompilerParams(
            collective_id=0, has_side_effects=True, vmem_limit_bytes=67043328
        ),
        name="routed_backward",
    )(
        cotangent,
        hidden.reshape(pair, slots, units),
        down_weight,
        routes.T,
        gate_prob.astype(F32).T,
        sign_seed.reshape(16, 128),
    )
    return (
        grad_hidden.reshape(hidden.shape),
        grad_prob.T,
        grad_weight.reshape(256, pair, units),
    )


def solution(mesh):
    in_specs = (
        P(("dp", "expert"), None),
        P(("dp", "expert"), None),
        P(("dp", "expert"), None),
        P("dp", "expert", None, None, None),
        P("expert", None, None),
        P(),
    )
    out_specs = (
        P("dp", "expert", None, None, None),
        P(("dp", "expert"), None),
        P("dp", "expert", None),
    )
    return jax.shard_map(shards, mesh=mesh, in_specs=in_specs, out_specs=out_specs, check_vma=False)
```

```python
import functools
import math

import jax
import jax.numpy as jnp
from jax import lax
from jax.experimental import pallas as pl
from jax.experimental.pallas import tpu as pltpu
from jax.sharding import PartitionSpec as P

MESH = pl.DeviceIdType.MESH
BLOCK = 128
NX, NY, NZ = 4, 4, 8
CH = 8
LANES = 128
CW = 2 * LANES
MISS = -100.0
BF16, F32 = jnp.bfloat16, jnp.float32


def dot_nn(a, b):
    return lax.dot_general(a, b, (((1,), (0,)), ((), ())), preferred_element_type=F32)


def dot_nt(a, b):
    return lax.dot_general(a, b, (((1,), (1,)), ((), ())), preferred_element_type=F32)


def kernel(
    cot, hid_hbm, w_hbm, routes_t, gate_t, seed,
    gh_out, gp_out, gw_out,
    zbuf, sel, rg, xsend, relay, wbuf, hid, weighted_t, acc, gh_buf, gw_buf,
    part, part_in, y_relay, y_fin,
    table, t_rows, x_rows, x_out, d_in, d_tab,
    r_tab, r_mid, r_out, r_end,
    load_sem, w_sem, hid_sem, out_sem,
    zs_sem, z_recv, tz_sem, tz_half, tz_recv,
    xs_sem, x_recv, xrel_recv, tx_sem, tx_recv,
    p_send, p_recv, yr_send, yr_recv, yf_send, yf_recv,
    rx_send, rx_recv, rz_send, rz_recv,
):
    rows48 = 48
    dp = lax.axis_index("dp")
    ex = lax.axis_index("expert")
    y, core = dp // 2, lax.rem(dp, 2)
    x, z = ex // NZ, lax.rem(ex, NZ)
    up = lambda v, d, n: lax.rem(v + d, n)

    def x_dev(xx):
        return (dp, xx * NZ + z)

    def z_dev(zz):
        return (dp, x * NZ + zz)

    xr, xl = x_dev(up(x, 1, NX)), x_dev(up(x, NX - 1, NX))
    zr, zl = z_dev(up(z, 1, NZ)), z_dev(up(z, NZ - 1, NZ))
    yr, yl = (up(y, 1, NY) * 2 + core, ex), (up(y, NY - 1, NY) * 2 + core, ex)
    partner = (y * 2 + 1 - core, ex)

    def remote(src, dst, send, recv, dev):
        return pltpu.make_async_remote_copy(
            src_ref=src, dst_ref=dst, send_sem=send, recv_sem=recv,
            device_id=dev, device_id_type=MESH,
        )

    def wait_recv(dst, sem):
        remote(dst, dst, sem, sem, xr).wait_recv()

    def wait_send(src, sem):
        remote(src, src, sem, sem, xr).wait_send()

    barrier = pltpu.get_barrier_semaphore()
    peers = [zr, zl, yr, yl, partner]
    peers += [x_dev(up(x, d, NX)) for d in range(1, NX)]
    for peer in peers:
        pl.semaphore_signal(barrier, inc=1, device_id=peer, device_id_type=MESH)

    def base_of(c, k):
        return 512 * ((c + 2 * k) % NY) + 256 * k + LANES * (c // NY)

    for c in range(CH):
        for k in range(2):
            pltpu.make_async_copy(
                cot.at[:, pl.ds(base_of(c, k), LANES)],
                zbuf.at[c, z, :, pl.ds(LANES * k, LANES)], load_sem,
            ).start()
    pltpu.make_async_copy(hid_hbm, hid, hid_sem).start()
    for c in range(CH):
        for k in range(2):
            pltpu.make_async_copy(
                w_hbm.at[:, :, pl.ds(base_of(c, k), LANES)],
                wbuf.at[c, :, :, pl.ds(LANES * k, LANES)], w_sem,
            ).start()

    e_iota = lax.broadcasted_iota(jnp.int32, (64, LANES), 0)
    gates = gate_t[...].astype(F32)
    hit = jnp.zeros((64, LANES), F32)
    gate = jnp.zeros((64, LANES), F32)
    for k in range(8):
        eq = routes_t[k:k + 1, :] == e_iota
        hit = jnp.where(eq, 1.0, hit)
        gate = jnp.where(eq, gates[k:k + 1, :], gate)
    earlier = (
        lax.broadcasted_iota(jnp.int32, (LANES, LANES), 0)
        < lax.broadcasted_iota(jnp.int32, (LANES, LANES), 1)
    )
    rank = dot_nn(hit.astype(BF16), jnp.where(earlier, 1.0, 0.0).astype(BF16))
    table[z, 0:64, :] = jnp.where(hit > 0.5, rank, MISS).astype(BF16)
    table[z, 64:128, :] = gate.astype(BF16)
    pltpu.make_async_copy(zbuf.at[:, z], zbuf.at[:, z], load_sem).wait()
    pl.semaphore_wait(barrier, len(peers))

    lower, upper = pl.ds(0, 64), pl.ds(64, 64)

    def z_send(c, h):
        right, left = up(z, NZ - h, NZ), up(z, h, NZ)
        if h < 3:
            remote(zbuf.at[c, right], zbuf.at[c, right], zs_sem.at[0], z_recv.at[c, h], zr).start()
            remote(zbuf.at[c, left], zbuf.at[c, left], zs_sem.at[1], z_recv.at[c, h], zl).start()
        else:
            remote(zbuf.at[c, right, lower], zbuf.at[c, right, lower], zs_sem.at[0], z_recv.at[c, h], zr).start()
            remote(zbuf.at[c, left, upper], zbuf.at[c, left, upper], zs_sem.at[1], z_recv.at[c, h], zl).start()

    def z_wait(c, dist):
        wait_recv(zbuf.at[c, pl.ds(0, 2 if dist < 4 else 1)], z_recv.at[c, dist - 1])

    def z_relay(c, h):
        if h > 0:
            z_wait(c, h)
        z_send(c, h)

    def table_send(h):
        right, left = up(z, NZ - h, NZ), up(z, h, NZ)
        if h < 3:
            remote(table.at[right], table.at[right], tz_sem.at[0], tz_recv.at[h], zr).start()
            remote(table.at[left], table.at[left], tz_sem.at[1], tz_recv.at[h], zl).start()
        else:
            remote(table.at[right, lower], table.at[right, lower], tz_half.at[0], tz_recv.at[h], zr).start()
            remote(table.at[left, upper], table.at[left, upper], tz_half.at[1], tz_recv.at[h], zl).start()

    def table_rows(zs):
        block = table[zs].astype(F32)
        t_rows[zs] = block

    def table_wait(dist):
        wait_recv(table.at[pl.ds(0, 2 if dist < 4 else 1)], tz_recv.at[dist - 1])
        if dist < 4:
            table_send(dist)
            table_rows(up(z, NZ - dist, NZ))
        table_rows(up(z, dist, NZ))

    table_send(0)
    z_send(0, 0)
    z_send(1, 0)
    table_rows(z)

    r_iota = lax.broadcasted_iota(jnp.int32, (rows48, LANES), 0).astype(F32)

    def one_hot_pair(even_row, odd_row):
        return even_row == r_iota, odd_row + 24.0 == r_iota

    def build_sel(m):
        for dx in range(NX):
            xx = up(x, dx, NX)
            for j in range(2):
                row = pl.ds(16 * xx + 2 * z + j, 1)
                even, odd = one_hot_pair(t_rows[2 * m, row, :], t_rows[2 * m + 1, row, :])
                at = (dx * 2 + j) * rows48
                sel[m, at:at + rows48, 0:LANES] = jnp.where(even, 1.0, 0.0).astype(BF16)
                sel[m, at:at + rows48, LANES:2 * LANES] = jnp.where(odd, 1.0, 0.0).astype(BF16)

    def x_tables():
        for xx in range(NX):
            row = 16 * xx + 2 * z
            for zs in range(NZ):
                for j in range(2):
                    at = 2 * zs + j
                    x_rows[xx, at:at + 1, :] = t_rows[zs, pl.ds(row + j, 1), :]
                    x_rows[xx, 16 + at:17 + at, :] = t_rows[zs, pl.ds(64 + row + j, 1), :]
            x_out[xx] = x_rows[xx].astype(BF16)
        for d in range(1, NX):
            to = up(x, d, NX)
            remote(x_out.at[to], d_in.at[x], tx_sem, tx_recv, x_dev(to)).start()
        d_in[x] = x_out[x]

    step_sign = 2 * lax.rem(z, 2) - 1

    def pair_of(i):
        turn = jnp.where(i == 0, 0, jnp.where(i == 1, 4 + step_sign, jnp.where(i == 2, 4 - step_sign, 2)))
        return lax.rem(z // 2 + turn, 4)

    def step_of(s, t):
        if t < 0:
            s, t = s - 1, t + 8
        tail = s == 3
        return (
            jnp.where(tail, 6 + t // 4, 2 * s + t % 2),
            jnp.where(tail, t % 4, t // 2),
        )

    def x_step(c, i):
        m = pair_of(i)
        tokens = zbuf[c, pl.ds(2 * m, 2)].reshape(2 * LANES, CW)
        rows = dot_nn(sel[m], tokens).astype(BF16)
        xsend[c, i] = rows[96:384].reshape(3, 2, rows48, CW)
        here = x * 4 + m
        remote(xsend.at[c, i, 1, 0], relay.at[c, i, 0], xs_sem.at[2], xrel_recv.at[c, i], xr).start()
        remote(xsend.at[c, i, 1, 1], relay.at[c, i, 1], xs_sem.at[3], xrel_recv.at[c, i], xl).start()
        remote(xsend.at[c, i, 0], rg.at[c, :, here], xs_sem.at[0], x_recv.at[c], xr).start()
        remote(xsend.at[c, i, 2], rg.at[c, :, here], xs_sem.at[1], x_recv.at[c], xl).start()
        rg[c, :, here] = rows[0:96].reshape(2, rows48, CW)

    def x_forward(c, i):
        m = pair_of(i)
        from_l, from_r = up(x, NX - 1, NX) * 4 + m, up(x, 1, NX) * 4 + m
        wait_recv(relay.at[c, i], xrel_recv.at[c, i])
        remote(relay.at[c, i, 0], rg.at[c, 0, from_l], xs_sem.at[4], x_recv.at[c], xr).start()
        remote(relay.at[c, i, 1], rg.at[c, 1, from_r], xs_sem.at[5], x_recv.at[c], xl).start()

    def x_wait(c):
        wait_recv(rg.at[c, :, pl.ds(0, 12)], x_recv.at[c])

    def pair_rows(p, j, row):
        xs, at = p // 4, 4 * lax.rem(p, 4) + j + row
        return d_tab[xs, pl.ds(at, 1), :], d_tab[xs, pl.ds(at + 2, 1), :]

    def slot_prob(p, j):
        even, odd = one_hot_pair(*pair_rows(p, j, 0))
        g_even, g_odd = pair_rows(p, j, 16)
        picked = jnp.where(even, g_even, 0.0) + jnp.where(odd, g_odd, 0.0)
        return jnp.sum(picked, axis=1, keepdims=True)

    def weigh():
        wait_recv(d_in.at[pl.ds(0, 3)], tx_recv)
        d_tab[...] = d_in[...].astype(F32)
        pltpu.make_async_copy(hid_hbm, hid, hid_sem).wait()

        def body(p, _):
            at = pl.ds(pl.multiple_of(p * rows48, 16), rows48)
            for j in range(2):
                rows = slot_prob(p, j) * hid[j, at, :].astype(F32)
                gh_buf[j, at, :] = rows.astype(BF16)
            return 0

        lax.fori_loop(0, 16, body, 0)
        for j in range(2):
            for q in range(6):
                cols = slice(LANES * q, LANES * (q + 1))
                weighted_t[j, cols, :] = gh_buf[j, :, cols].T

    def partial(c):
        for j in range(2):
            for q in range(3):
                fs = slice(256 * q, 256 * (q + 1))
                got = dot_nn(weighted_t[j, fs, :], rg[c, j].reshape(768, CW)).astype(BF16)
                for k in range(2):
                    part[c, k, j, fs, :] = got[:, LANES * k:LANES * (k + 1)]
            remote(part.at[c, 1 - core, j], part_in.at[c, j], p_send, p_recv.at[c], partner).start()

    def back(c):
        for j in range(2):
            for q in range(3):
                rs = slice(256 * q, 256 * (q + 1))
                acc[j, rs, :] += dot_nt(rg[c, j].reshape(768, CW)[rs], wbuf[c, j])

    def role(c):
        return up(y + NY, NY - lax.rem(c + 2 * core, NY), NY)

    def pair_add(c):
        half, at = c // NY, role(c)
        wait_recv(part_in.at[c], p_recv.at[c])
        for j in range(2):
            total = part[c, core, j].astype(F32) + part_in[c, j].astype(F32)
            part[c, core, j] = total.astype(BF16)
        mine = part.at[c, core]

        @pl.when(at == 2)
        def _():
            remote(mine.at[0], y_relay.at[half, 0], yr_send, yr_recv.at[half, 0], yr).start()
            remote(mine.at[1], y_relay.at[half, 1], yr_send, yr_recv.at[half, 1], yl).start()

        @pl.when(at == 3)
        def _():
            remote(mine.at[1], y_fin.at[half, 0, 1], yf_send, yf_recv.at[half], yr).start()

        @pl.when(at == 1)
        def _():
            remote(mine.at[0], y_fin.at[half, 1, 0], yf_send, yf_recv.at[half], yl).start()

    def relay_add(c):
        half, at = c // NY, role(c)
        for j, place, side, dev in ((0, 3, 0, yr), (1, 1, 1, yl)):
            @pl.when(at == place)
            def _(j=j, side=side, dev=dev):
                wait_recv(y_relay.at[half, j], yr_recv.at[half, j])
                total = part[c, core, j].astype(F32) + y_relay[half, j].astype(F32)
                part[c, core, j] = total.astype(BF16)
                remote(part.at[c, core, j], y_fin.at[half, side, j], yf_send, yf_recv.at[half], dev).start()

    def finish(c):
        half = c // NY

        @pl.when(role(c) == 0)
        def _():
            i0 = lax.broadcasted_iota(jnp.int32, (BLOCK, BLOCK), 0)
            i1 = lax.broadcasted_iota(jnp.int32, (BLOCK, BLOCK), 1)
            bits = i0 & i1
            bits = bits ^ (bits >> 4)
            bits = bits ^ (bits >> 2)
            bits = bits ^ (bits >> 1)
            sign = (2 * seed[pl.ds(4 * y + 2 * core + half, 1), :] - 1).astype(F32)
            turn = (jnp.where((bits & 1) == 1, -1.0, 1.0) * sign).astype(BF16)
            out_rows = pl.ds(pl.multiple_of(half * BLOCK, BLOCK), BLOCK)
            wait_recv(y_fin.at[half], yf_recv.at[half])
            for j in range(2):
                total = part[c, core, j].astype(F32) + y_fin[half, 0, j].astype(F32) + y_fin[half, 1, j].astype(F32)
                high = total.astype(BF16)
                low = (total - high.astype(F32)).astype(BF16)
                turned = (dot_nt(turn, high) + dot_nt(turn, low)) * (1.0 / math.sqrt(BLOCK))
                gw_buf[out_rows, 768 * j:768 * (j + 1)] = turned
            pltpu.make_async_copy(gw_buf.at[out_rows], gw_out.at[out_rows], out_sem.at[half]).start()

    acc[...] = jnp.zeros(acc.shape, F32)

    def double(s, _):
        first, more = s == 0, s > 0
        for t in range(8):
            q, h = t % 2, t // 2

            @pl.when(first)
            def _(q=q, h=h):
                z_wait(q, h + 1)
                if h < 3:
                    z_send(q, h + 1)
                if q == 0:
                    table_wait(h + 1)
                    build_sel(pair_of(h))

            if t in (0, 1, 2):
                @pl.when(more)
                def _(t=t):
                    if t == 0:
                        z_relay(2 * s + 1, 2)
                    else:
                        z_relay(2 * s + t - 1, 3)
            else:
                @pl.when(s < 3)
                def _(t=t):
                    z_relay(2 * s + 2 + (t - 3) % 2, (t - 3) // 2)

            c, i = step_of(s, t)
            if t in (3, 6, 7):
                @pl.when(more & (i == 3))
                def _(c=c):
                    z_wait(c, 4)
            x_step(c, i)
            fc, fi = step_of(s, t - 3)
            if t < 3:
                @pl.when(more)
                def _(fc=fc, fi=fi):
                    x_forward(fc, fi)
            else:
                x_forward(fc, fi)

            a, b = 2 * s - 2, 2 * s - 1
            if t == 2:
                @pl.when(s == 1)
                def _():
                    weigh()
            if t in (1, 2):
                @pl.when(s > 1)
                def _(t=t):
                    finish(2 * s - 5 + t)
            if t == 3:
                @pl.when(more)
                def _():
                    x_wait(a)
                    partial(a)
            if t == 4:
                @pl.when(more)
                def _():
                    x_wait(b)
                    partial(b)
            if t == 5:
                @pl.when(s == 1)
                def _():
                    pltpu.make_async_copy(wbuf, wbuf, w_sem).wait()

                @pl.when(more)
                def _():
                    back(a)
                    pair_add(a)
            if t == 6:
                @pl.when(more)
                def _():
                    back(b)
                    pair_add(b)
            if t == 7:
                @pl.when(first)
                def _():
                    x_tables()

                @pl.when(more)
                def _():
                    relay_add(a)
                    relay_add(b)
        return 0

    lax.fori_loop(0, CH // 2, double, 0)

    x_forward(7, 1)
    x_forward(7, 2)
    x_wait(6)
    partial(6)
    x_forward(7, 3)
    back(6)
    pair_add(6)
    finish(4)
    finish(5)
    x_wait(7)
    partial(7)
    back(7)
    pair_add(7)
    relay_add(6)

    def outputs(p, _):
        at = pl.ds(pl.multiple_of(p * rows48, 16), rows48)
        xs, row = p // 4, 4 * lax.rem(p, 4)
        for j in range(2):
            rows = acc[j, at, :]
            gh_buf[j, at, :] = (slot_prob(p, j) * rows).astype(BF16)
            slot = jnp.sum(rows * hid[j, at, :].astype(F32), axis=1, keepdims=True)
            even, odd = one_hot_pair(*pair_rows(p, j, 0))
            r_tab[xs, pl.ds(row + j, 1), :] = jnp.sum(jnp.where(even, slot, 0.0), axis=0, keepdims=True)
            r_tab[xs, pl.ds(row + 2 + j, 1), :] = jnp.sum(jnp.where(odd, slot, 0.0), axis=0, keepdims=True)
        return 0

    lax.fori_loop(0, 8, outputs, 0)
    relay_add(7)
    lax.fori_loop(8, 16, outputs, 0)

    for d in range(1, NX):
        to = up(x, d, NX)
        remote(r_tab.at[to], r_mid.at[x], rx_send, rx_recv, x_dev(to)).start()
    r_mid[x] = r_tab[x]
    pltpu.make_async_copy(gh_buf, gh_out, hid_sem).start()
    finish(6)
    wait_recv(r_mid.at[pl.ds(0, 3)], rx_recv)
    for zs in range(NZ):
        for xx in range(NX):
            r_out[zs, 2 * xx:2 * xx + 2, :] = r_mid[xx, 2 * zs:2 * zs + 2, :]
    for d in range(1, NZ):
        to = up(z, d, NZ)
        remote(r_out.at[to], r_end.at[z], rz_send, rz_recv, z_dev(to)).start()
    r_end[z] = r_out[z]
    finish(7)
    wait_recv(r_end.at[pl.ds(0, 7)], rz_recv)
    grad_prob = jnp.zeros((8, LANES), F32)
    chosen = routes_t[...]
    for zz in range(NZ):
        for xx in range(NX):
            for j in range(2):
                e = 16 * xx + 2 * zz + j
                row = 2 * xx + j
                grad_prob = jnp.where(chosen == e, r_end[zz, row:row + 1, :], grad_prob)
    gp_out[...] = grad_prob

    wait_send(zbuf.at[pl.ds(0, 4), pl.ds(0, 7)], zs_sem.at[0])
    wait_send(zbuf.at[pl.ds(0, 4), pl.ds(0, 7)], zs_sem.at[1])
    for side in range(2):
        wait_send(table.at[pl.ds(0, 3)], tz_sem.at[side])
        wait_send(table.at[0, lower], tz_half.at[side])
        wait_send(xsend.at[:, :, 2 * side], xs_sem.at[side])
        wait_send(xsend.at[:, :, 1, side], xs_sem.at[2 + side])
        wait_send(relay.at[:, :, side], xs_sem.at[4 + side])
    wait_send(x_out.at[pl.ds(0, 3)], tx_sem)
    wait_send(r_tab.at[pl.ds(0, 3)], rx_send)
    wait_send(r_out.at[pl.ds(0, 7)], rz_send)
    wait_send(part.at[:, 0], p_send)
    wait_send(part.at[pl.ds(0, 2), 0], yr_send)
    wait_send(part.at[pl.ds(0, 4), 0], yf_send)
    pltpu.make_async_copy(gh_buf, gh_out, hid_sem).wait()
    for half in range(2):
        out_rows = pl.ds(BLOCK * half, BLOCK)
        pltpu.make_async_copy(gw_buf.at[out_rows], gw_out.at[out_rows], out_sem.at[half]).wait()


def shards(cotangent, gate_prob, routes, hidden, down_weight, sign_seed):
    tok, features = cotangent.shape
    _, pair, sources, cap, units = hidden.shape
    slots = sources * cap
    vm = pl.BlockSpec(memory_space=pltpu.VMEM)
    anyspec = pl.BlockSpec(memory_space=pl.ANY)
    dma = pltpu.SemaphoreType.DMA
    scratch = [
        pltpu.VMEM((CH, NZ, tok, CW), BF16),
        pltpu.VMEM((4, 384, 256), BF16),
        pltpu.VMEM((CH, 2, 16, 48, CW), BF16),
        pltpu.VMEM((CH, 4, 3, 2, 48, CW), BF16),
        pltpu.VMEM((CH, 4, 2, 48, CW), BF16),
        pltpu.VMEM((CH, 2, units, CW), BF16),
        pltpu.VMEM((2, slots, units), BF16),
        pltpu.VMEM((2, units, slots), BF16),
        pltpu.VMEM((2, slots, units), F32),
        pltpu.VMEM((2, slots, units), BF16),
        pltpu.VMEM((256, pair * units), F32),
        pltpu.VMEM((CH, 2, 2, units, LANES), BF16),
        pltpu.VMEM((CH, 2, units, LANES), BF16),
        pltpu.VMEM((2, 2, units, LANES), BF16),
        pltpu.VMEM((2, 2, 2, units, LANES), BF16),
        pltpu.VMEM((NZ, 128, LANES), BF16),
        pltpu.VMEM((NZ, 128, LANES), F32),
        pltpu.VMEM((NX, 32, LANES), F32),
        pltpu.VMEM((NX, 32, LANES), BF16),
        pltpu.VMEM((NX, 32, LANES), BF16),
        pltpu.VMEM((NX, 32, LANES), F32),
        pltpu.VMEM((NX, 16, LANES), F32),
        pltpu.VMEM((NX, 16, LANES), F32),
        pltpu.VMEM((NZ, 8, LANES), F32),
        pltpu.VMEM((NZ, 8, LANES), F32),
        dma, dma, dma, dma((2,)),
        dma((2,)), dma((CH, 4)),
        dma((2,)), dma((2,)), dma((4,)),
        dma((6,)), dma((CH,)), dma((CH, 4)),
        dma, dma,
        dma, dma((CH,)),
        dma, dma((2, 2)), dma, dma((2,)),
        dma, dma, dma, dma,
    ]
    grad_hidden, grad_prob, grad_weight = pl.pallas_call(
        kernel,
        out_shape=(
            jax.ShapeDtypeStruct((pair, slots, units), BF16),
            jax.ShapeDtypeStruct((8, tok), F32),
            jax.ShapeDtypeStruct((256, pair * units), F32),
        ),
        in_specs=[anyspec, anyspec, anyspec, vm, vm, vm],
        out_specs=(anyspec, vm, anyspec),
        scratch_shapes=scratch,
        compiler_params=pltpu.CompilerParams(
            collective_id=0, has_side_effects=True, vmem_limit_bytes=67043328
        ),
        name="routed_backward",
    )(
        cotangent,
        hidden.reshape(pair, slots, units),
        down_weight,
        routes.T,
        gate_prob.T,
        sign_seed.reshape(16, 128),
    )
    return (
        grad_hidden.reshape(hidden.shape),
        grad_prob.T,
        grad_weight.reshape(256, pair, units),
    )


def solution(mesh):
    in_specs = (
        P(("dp", "expert"), None),
        P(("dp", "expert"), None),
        P(("dp", "expert"), None),
        P("dp", "expert", None, None, None),
        P("expert", None, None),
        P(),
    )
    out_specs = (
        P("dp", "expert", None, None, None),
        P(("dp", "expert"), None),
        P("dp", "expert", None),
    )
    return jax.shard_map(shards, mesh=mesh, in_specs=in_specs, out_specs=out_specs, check_vma=False)
```

```python
import functools
import math

import jax
import jax.numpy as jnp
from jax import lax
from jax.experimental import pallas as pl
from jax.experimental.pallas import tpu as pltpu
from jax.sharding import PartitionSpec as P

MESH = pl.DeviceIdType.MESH
BLOCK = 128
NX, NY, NZ = 4, 4, 8
CH = 8
LANES = 128
CW = 2 * LANES
MISS = -100.0
BF16, F32 = jnp.bfloat16, jnp.float32


def dot_nn(a, b):
    return lax.dot_general(a, b, (((1,), (0,)), ((), ())), preferred_element_type=F32)


def dot_nt(a, b):
    return lax.dot_general(a, b, (((1,), (1,)), ((), ())), preferred_element_type=F32)


def kernel(
    cot, hid_hbm, w_hbm, routes_t, gate_t, seed,
    gh_out, gp_out, gw_out,
    zbuf, sel, rg, xsend, relay, wbuf, hid, weighted_t, acc, gh_buf, gw_buf,
    part, part_in, y_relay, y_fin,
    table, t_rows, x_rows, x_out, d_in, d_tab,
    r_tab, r_mid, r_out, r_end,
    load_sem, w_sem, hid_sem, out_sem,
    zs_sem, z_recv, tz_sem, tz_half, tz_recv,
    xs_sem, x_recv, xrel_recv, tx_sem, tx_recv,
    p_send, p_recv, yr_send, yr_recv, yf_send, yf_recv,
    rx_send, rx_recv, rz_send, rz_recv,
):
    rows48 = 48
    dp = lax.axis_index("dp")
    ex = lax.axis_index("expert")
    y, core = dp // 2, lax.rem(dp, 2)
    x, z = ex // NZ, lax.rem(ex, NZ)
    up = lambda v, d, n: lax.rem(v + d, n)

    def x_dev(xx):
        return (dp, xx * NZ + z)

    def z_dev(zz):
        return (dp, x * NZ + zz)

    xr, xl = x_dev(up(x, 1, NX)), x_dev(up(x, NX - 1, NX))
    zr, zl = z_dev(up(z, 1, NZ)), z_dev(up(z, NZ - 1, NZ))
    yr, yl = (up(y, 1, NY) * 2 + core, ex), (up(y, NY - 1, NY) * 2 + core, ex)
    partner = (y * 2 + 1 - core, ex)

    def remote(src, dst, send, recv, dev):
        return pltpu.make_async_remote_copy(
            src_ref=src, dst_ref=dst, send_sem=send, recv_sem=recv,
            device_id=dev, device_id_type=MESH,
        )

    def wait_recv(dst, sem):
        remote(dst, dst, sem, sem, xr).wait_recv()

    def wait_send(src, sem):
        remote(src, src, sem, sem, xr).wait_send()

    barrier = pltpu.get_barrier_semaphore()
    peers = [zr, zl, yr, yl, partner]
    peers += [x_dev(up(x, d, NX)) for d in range(1, NX)]
    for peer in peers:
        pl.semaphore_signal(barrier, inc=1, device_id=peer, device_id_type=MESH)

    def base_of(c, k):
        return 512 * ((c + 2 * k) % NY) + 256 * k + LANES * (c // NY)

    for c in range(CH):
        for k in range(2):
            pltpu.make_async_copy(
                cot.at[:, pl.ds(base_of(c, k), LANES)],
                zbuf.at[c, z, :, pl.ds(LANES * k, LANES)], load_sem,
            ).start()
    pltpu.make_async_copy(hid_hbm, hid, hid_sem).start()
    for c in range(CH):
        for k in range(2):
            pltpu.make_async_copy(
                w_hbm.at[:, :, pl.ds(base_of(c, k), LANES)],
                wbuf.at[c, :, :, pl.ds(LANES * k, LANES)], w_sem,
            ).start()

    e_iota = lax.broadcasted_iota(jnp.int32, (64, LANES), 0)
    gates = gate_t[...].astype(F32)
    hit = jnp.zeros((64, LANES), F32)
    gate = jnp.zeros((64, LANES), F32)
    for k in range(8):
        eq = routes_t[k:k + 1, :] == e_iota
        hit = jnp.where(eq, 1.0, hit)
        gate = jnp.where(eq, gates[k:k + 1, :], gate)
    earlier = (
        lax.broadcasted_iota(jnp.int32, (LANES, LANES), 0)
        < lax.broadcasted_iota(jnp.int32, (LANES, LANES), 1)
    )
    rank = dot_nn(hit.astype(BF16), jnp.where(earlier, 1.0, 0.0).astype(BF16))
    table[z, 0:64, :] = jnp.where(hit > 0.5, rank, MISS).astype(BF16)
    table[z, 64:128, :] = gate.astype(BF16)
    pltpu.make_async_copy(zbuf.at[:, z], zbuf.at[:, z], load_sem).wait()
    pl.semaphore_wait(barrier, len(peers))

    lower, upper = pl.ds(0, 64), pl.ds(64, 64)

    def z_send(c, h):
        right, left = up(z, NZ - h, NZ), up(z, h, NZ)
        if h < 3:
            remote(zbuf.at[c, right], zbuf.at[c, right], zs_sem.at[0], z_recv.at[c, h], zr).start()
            remote(zbuf.at[c, left], zbuf.at[c, left], zs_sem.at[1], z_recv.at[c, h], zl).start()
        else:
            remote(zbuf.at[c, right, lower], zbuf.at[c, right, lower], zs_sem.at[0], z_recv.at[c, h], zr).start()
            remote(zbuf.at[c, left, upper], zbuf.at[c, left, upper], zs_sem.at[1], z_recv.at[c, h], zl).start()

    def z_wait(c, dist):
        wait_recv(zbuf.at[c, pl.ds(0, 2 if dist < 4 else 1)], z_recv.at[c, dist - 1])

    def z_relay(c, h):
        if h > 0:
            z_wait(c, h)
        z_send(c, h)

    def table_send(h):
        right, left = up(z, NZ - h, NZ), up(z, h, NZ)
        if h < 3:
            remote(table.at[right], table.at[right], tz_sem.at[0], tz_recv.at[h], zr).start()
            remote(table.at[left], table.at[left], tz_sem.at[1], tz_recv.at[h], zl).start()
        else:
            remote(table.at[right, lower], table.at[right, lower], tz_half.at[0], tz_recv.at[h], zr).start()
            remote(table.at[left, upper], table.at[left, upper], tz_half.at[1], tz_recv.at[h], zl).start()

    def table_rows(zs):
        block = table[zs].astype(F32)
        t_rows[zs] = block

    def table_wait(dist):
        wait_recv(table.at[pl.ds(0, 2 if dist < 4 else 1)], tz_recv.at[dist - 1])
        if dist < 4:
            table_send(dist)
            table_rows(up(z, NZ - dist, NZ))
        table_rows(up(z, dist, NZ))

    table_send(0)
    z_send(0, 0)
    z_send(1, 0)
    table_rows(z)

    r_iota = lax.broadcasted_iota(jnp.int32, (rows48, LANES), 0).astype(F32)

    def one_hot_pair(even_row, odd_row):
        return even_row == r_iota, odd_row + 24.0 == r_iota

    def build_sel(m):
        for dx in range(NX):
            xx = up(x, dx, NX)
            for j in range(2):
                row = pl.ds(16 * xx + 2 * z + j, 1)
                even, odd = one_hot_pair(t_rows[2 * m, row, :], t_rows[2 * m + 1, row, :])
                at = (dx * 2 + j) * rows48
                sel[m, at:at + rows48, 0:LANES] = jnp.where(even, 1.0, 0.0).astype(BF16)
                sel[m, at:at + rows48, LANES:2 * LANES] = jnp.where(odd, 1.0, 0.0).astype(BF16)

    def x_tables():
        for xx in range(NX):
            row = 16 * xx + 2 * z
            for zs in range(NZ):
                for j in range(2):
                    at = 2 * zs + j
                    x_rows[xx, at:at + 1, :] = t_rows[zs, pl.ds(row + j, 1), :]
                    x_rows[xx, 16 + at:17 + at, :] = t_rows[zs, pl.ds(64 + row + j, 1), :]
            x_out[xx] = x_rows[xx].astype(BF16)
        for d in range(1, NX):
            to = up(x, d, NX)
            remote(x_out.at[to], d_in.at[x], tx_sem, tx_recv, x_dev(to)).start()
        d_in[x] = x_out[x]

    step_sign = 2 * lax.rem(z, 2) - 1

    def pair_of(i):
        turn = jnp.where(i == 0, 0, jnp.where(i == 1, 4 + step_sign, jnp.where(i == 2, 4 - step_sign, 2)))
        return lax.rem(z // 2 + turn, 4)

    def step_of(s, t):
        if t < 0:
            s, t = s - 1, t + 8
        tail = s >= 1
        return (
            jnp.where(tail, 2 * s + t // 4, 2 * s + t % 2),
            jnp.where(tail, t % 4, t // 2),
        )

    def x_step(c, i):
        m = pair_of(i)
        tokens = zbuf[c, pl.ds(2 * m, 2)].reshape(2 * LANES, CW)
        rows = dot_nn(sel[m], tokens).astype(BF16)
        xsend[c, i] = rows[96:384].reshape(3, 2, rows48, CW)
        here = x * 4 + m
        remote(xsend.at[c, i, 1, 0], relay.at[c, i, 0], xs_sem.at[2], xrel_recv.at[c, i], xr).start()
        remote(xsend.at[c, i, 1, 1], relay.at[c, i, 1], xs_sem.at[3], xrel_recv.at[c, i], xl).start()
        remote(xsend.at[c, i, 0], rg.at[c, :, here], xs_sem.at[0], x_recv.at[c], xr).start()
        remote(xsend.at[c, i, 2], rg.at[c, :, here], xs_sem.at[1], x_recv.at[c], xl).start()
        rg[c, :, here] = rows[0:96].reshape(2, rows48, CW)

    def x_forward(c, i):
        m = pair_of(i)
        from_l, from_r = up(x, NX - 1, NX) * 4 + m, up(x, 1, NX) * 4 + m
        wait_recv(relay.at[c, i], xrel_recv.at[c, i])
        remote(relay.at[c, i, 0], rg.at[c, 0, from_l], xs_sem.at[4], x_recv.at[c], xr).start()
        remote(relay.at[c, i, 1], rg.at[c, 1, from_r], xs_sem.at[5], x_recv.at[c], xl).start()

    def x_wait(c):
        wait_recv(rg.at[c, :, pl.ds(0, 12)], x_recv.at[c])

    def pair_rows(p, j, row):
        xs, at = p // 4, 4 * lax.rem(p, 4) + j + row
        return d_tab[xs, pl.ds(at, 1), :], d_tab[xs, pl.ds(at + 2, 1), :]

    def slot_prob(p, j):
        even, odd = one_hot_pair(*pair_rows(p, j, 0))
        g_even, g_odd = pair_rows(p, j, 16)
        picked = jnp.where(even, g_even, 0.0) + jnp.where(odd, g_odd, 0.0)
        return jnp.sum(picked, axis=1, keepdims=True)

    def weigh():
        wait_recv(d_in.at[pl.ds(0, 3)], tx_recv)
        d_tab[...] = d_in[...].astype(F32)
        pltpu.make_async_copy(hid_hbm, hid, hid_sem).wait()

        def body(p, _):
            at = pl.ds(pl.multiple_of(p * rows48, 16), rows48)
            for j in range(2):
                rows = slot_prob(p, j) * hid[j, at, :].astype(F32)
                gh_buf[j, at, :] = rows.astype(BF16)
            return 0

        lax.fori_loop(0, 16, body, 0)
        for j in range(2):
            for q in range(6):
                cols = slice(LANES * q, LANES * (q + 1))
                weighted_t[j, cols, :] = gh_buf[j, :, cols].T

    def partial(c):
        for j in range(2):
            for q in range(3):
                fs = slice(256 * q, 256 * (q + 1))
                got = dot_nn(weighted_t[j, fs, :], rg[c, j].reshape(768, CW)).astype(BF16)
                for k in range(2):
                    part[c, k, j, fs, :] = got[:, LANES * k:LANES * (k + 1)]
            remote(part.at[c, 1 - core, j], part_in.at[c, j], p_send, p_recv.at[c], partner).start()

    def back(c):
        for j in range(2):
            for q in range(3):
                rs = slice(256 * q, 256 * (q + 1))
                acc[j, rs, :] += dot_nt(rg[c, j].reshape(768, CW)[rs], wbuf[c, j])

    def role(c):
        return up(y + NY, NY - lax.rem(c + 2 * core, NY), NY)

    def pair_add(c):
        half, at = c // NY, role(c)
        wait_recv(part_in.at[c], p_recv.at[c])
        for j in range(2):
            total = part[c, core, j].astype(F32) + part_in[c, j].astype(F32)
            part[c, core, j] = total.astype(BF16)
        mine = part.at[c, core]

        @pl.when(at == 2)
        def _():
            remote(mine.at[0], y_relay.at[half, 0], yr_send, yr_recv.at[half, 0], yr).start()
            remote(mine.at[1], y_relay.at[half, 1], yr_send, yr_recv.at[half, 1], yl).start()

        @pl.when(at == 3)
        def _():
            remote(mine.at[1], y_fin.at[half, 0, 1], yf_send, yf_recv.at[half], yr).start()

        @pl.when(at == 1)
        def _():
            remote(mine.at[0], y_fin.at[half, 1, 0], yf_send, yf_recv.at[half], yl).start()

    def relay_add(c):
        half, at = c // NY, role(c)
        for j, place, side, dev in ((0, 3, 0, yr), (1, 1, 1, yl)):
            @pl.when(at == place)
            def _(j=j, side=side, dev=dev):
                wait_recv(y_relay.at[half, j], yr_recv.at[half, j])
                total = part[c, core, j].astype(F32) + y_relay[half, j].astype(F32)
                part[c, core, j] = total.astype(BF16)
                remote(part.at[c, core, j], y_fin.at[half, side, j], yf_send, yf_recv.at[half], dev).start()

    def finish(c):
        half = c // NY

        @pl.when(role(c) == 0)
        def _():
            i0 = lax.broadcasted_iota(jnp.int32, (BLOCK, BLOCK), 0)
            i1 = lax.broadcasted_iota(jnp.int32, (BLOCK, BLOCK), 1)
            bits = i0 & i1
            bits = bits ^ (bits >> 4)
            bits = bits ^ (bits >> 2)
            bits = bits ^ (bits >> 1)
            sign = (2 * seed[pl.ds(4 * y + 2 * core + half, 1), :] - 1).astype(F32)
            turn = (jnp.where((bits & 1) == 1, -1.0, 1.0) * sign).astype(BF16)
            out_rows = pl.ds(pl.multiple_of(half * BLOCK, BLOCK), BLOCK)
            wait_recv(y_fin.at[half], yf_recv.at[half])
            for j in range(2):
                total = part[c, core, j].astype(F32) + y_fin[half, 0, j].astype(F32) + y_fin[half, 1, j].astype(F32)
                high = total.astype(BF16)
                low = (total - high.astype(F32)).astype(BF16)
                turned = (dot_nt(turn, high) + dot_nt(turn, low)) * (1.0 / math.sqrt(BLOCK))
                gw_buf[out_rows, 768 * j:768 * (j + 1)] = turned
            pltpu.make_async_copy(gw_buf.at[out_rows], gw_out.at[out_rows], out_sem.at[half]).start()

    acc[...] = jnp.zeros(acc.shape, F32)

    def double(s, _):
        first, more = s == 0, s > 0
        for t in range(8):
            q, h = t % 2, t // 2

            @pl.when(first)
            def _(q=q, h=h):
                z_wait(q, h + 1)
                if h < 3:
                    z_send(q, h + 1)
                if q == 0:
                    table_wait(h + 1)
                    build_sel(pair_of(h))

            if t in (0, 1, 2):
                @pl.when(more)
                def _(t=t):
                    if t == 0:
                        z_relay(2 * s + 1, 2)
                    else:
                        z_relay(2 * s + t - 1, 3)
            else:
                @pl.when(s < 3)
                def _(t=t):
                    z_relay(2 * s + 2 + (t - 3) % 2, (t - 3) // 2)

            c, i = step_of(s, t)
            if t in (3, 7):
                @pl.when(more)
                def _(c=c):
                    z_wait(c, 4)
            x_step(c, i)
            fc, fi = step_of(s, t - 3)
            if t < 3:
                @pl.when(more)
                def _(fc=fc, fi=fi):
                    x_forward(fc, fi)
            else:
                x_forward(fc, fi)

            at_one, later = s == 1, s > 1
            if t == 0:
                @pl.when(later)
                def _():
                    pair_add(2 * s - 3)
            if t == 2:
                @pl.when(at_one)
                def _():
                    weigh()

                @pl.when(later)
                def _():
                    x_wait(2 * s - 2)
                    partial(2 * s - 2)

                @pl.when(s == 2)
                def _():
                    relay_add(0)
            if t == 3:
                @pl.when(later)
                def _():
                    back(2 * s - 2)
                    relay_add(2 * s - 3)
            if t == 4:
                @pl.when(later)
                def _():
                    pair_add(2 * s - 2)
            if t == 5:
                @pl.when(at_one)
                def _():
                    pltpu.make_async_copy(wbuf, wbuf, w_sem).wait()
                    x_wait(0)
                    partial(0)
                    back(0)

                @pl.when(later)
                def _():
                    finish(jnp.where(s == 2, 0, 2))
            if t == 6:
                @pl.when(more)
                def _():
                    x_wait(2 * s - 1)
                    partial(2 * s - 1)
            if t == 7:
                @pl.when(first)
                def _():
                    x_tables()

                @pl.when(at_one)
                def _():
                    pair_add(0)

                @pl.when(more)
                def _():
                    back(2 * s - 1)

                @pl.when(later)
                def _():
                    relay_add(2 * s - 2)
                    finish(2 * s - 3)
        return 0

    lax.fori_loop(0, CH // 2, double, 0)

    x_forward(7, 1)
    x_forward(7, 2)
    pair_add(5)
    x_wait(6)
    partial(6)
    x_forward(7, 3)
    back(6)
    pair_add(6)
    relay_add(5)
    x_wait(7)
    partial(7)
    finish(4)
    pair_add(7)
    back(7)
    relay_add(6)
    finish(5)
    relay_add(7)

    def outputs(p, _):
        at = pl.ds(pl.multiple_of(p * rows48, 16), rows48)
        xs, row = p // 4, 4 * lax.rem(p, 4)
        for j in range(2):
            rows = acc[j, at, :]
            gh_buf[j, at, :] = (slot_prob(p, j) * rows).astype(BF16)
            slot = jnp.sum(rows * hid[j, at, :].astype(F32), axis=1, keepdims=True)
            even, odd = one_hot_pair(*pair_rows(p, j, 0))
            r_tab[xs, pl.ds(row + j, 1), :] = jnp.sum(jnp.where(even, slot, 0.0), axis=0, keepdims=True)
            r_tab[xs, pl.ds(row + 2 + j, 1), :] = jnp.sum(jnp.where(odd, slot, 0.0), axis=0, keepdims=True)
        return 0

    lax.fori_loop(0, 16, outputs, 0)

    for d in range(1, NX):
        to = up(x, d, NX)
        remote(r_tab.at[to], r_mid.at[x], rx_send, rx_recv, x_dev(to)).start()
    r_mid[x] = r_tab[x]
    pltpu.make_async_copy(gh_buf, gh_out, hid_sem).start()
    finish(6)
    wait_recv(r_mid.at[pl.ds(0, 3)], rx_recv)
    for zs in range(NZ):
        for xx in range(NX):
            r_out[zs, 2 * xx:2 * xx + 2, :] = r_mid[xx, 2 * zs:2 * zs + 2, :]
    for d in range(1, NZ):
        to = up(z, d, NZ)
        remote(r_out.at[to], r_end.at[z], rz_send, rz_recv, z_dev(to)).start()
    r_end[z] = r_out[z]
    finish(7)
    wait_recv(r_end.at[pl.ds(0, 7)], rz_recv)
    grad_prob = jnp.zeros((8, LANES), F32)
    chosen = routes_t[...]
    for zz in range(NZ):
        for xx in range(NX):
            for j in range(2):
                e = 16 * xx + 2 * zz + j
                row = 2 * xx + j
                grad_prob = jnp.where(chosen == e, r_end[zz, row:row + 1, :], grad_prob)
    gp_out[...] = grad_prob

    wait_send(zbuf.at[pl.ds(0, 4), pl.ds(0, 7)], zs_sem.at[0])
    wait_send(zbuf.at[pl.ds(0, 4), pl.ds(0, 7)], zs_sem.at[1])
    for side in range(2):
        wait_send(table.at[pl.ds(0, 3)], tz_sem.at[side])
        wait_send(table.at[0, lower], tz_half.at[side])
        wait_send(xsend.at[:, :, 2 * side], xs_sem.at[side])
        wait_send(xsend.at[:, :, 1, side], xs_sem.at[2 + side])
        wait_send(relay.at[:, :, side], xs_sem.at[4 + side])
    wait_send(x_out.at[pl.ds(0, 3)], tx_sem)
    wait_send(r_tab.at[pl.ds(0, 3)], rx_send)
    wait_send(r_out.at[pl.ds(0, 7)], rz_send)
    wait_send(part.at[:, 0], p_send)
    wait_send(part.at[pl.ds(0, 2), 0], yr_send)
    wait_send(part.at[pl.ds(0, 4), 0], yf_send)
    pltpu.make_async_copy(gh_buf, gh_out, hid_sem).wait()
    for half in range(2):
        out_rows = pl.ds(BLOCK * half, BLOCK)
        pltpu.make_async_copy(gw_buf.at[out_rows], gw_out.at[out_rows], out_sem.at[half]).wait()


def shards(cotangent, gate_prob, routes, hidden, down_weight, sign_seed):
    tok, features = cotangent.shape
    _, pair, sources, cap, units = hidden.shape
    slots = sources * cap
    vm = pl.BlockSpec(memory_space=pltpu.VMEM)
    anyspec = pl.BlockSpec(memory_space=pl.ANY)
    dma = pltpu.SemaphoreType.DMA
    scratch = [
        pltpu.VMEM((CH, NZ, tok, CW), BF16),
        pltpu.VMEM((4, 384, 256), BF16),
        pltpu.VMEM((CH, 2, 16, 48, CW), BF16),
        pltpu.VMEM((CH, 4, 3, 2, 48, CW), BF16),
        pltpu.VMEM((CH, 4, 2, 48, CW), BF16),
        pltpu.VMEM((CH, 2, units, CW), BF16),
        pltpu.VMEM((2, slots, units), BF16),
        pltpu.VMEM((2, units, slots), BF16),
        pltpu.VMEM((2, slots, units), F32),
        pltpu.VMEM((2, slots, units), BF16),
        pltpu.VMEM((256, pair * units), F32),
        pltpu.VMEM((CH, 2, 2, units, LANES), BF16),
        pltpu.VMEM((CH, 2, units, LANES), BF16),
        pltpu.VMEM((2, 2, units, LANES), BF16),
        pltpu.VMEM((2, 2, 2, units, LANES), BF16),
        pltpu.VMEM((NZ, 128, LANES), BF16),
        pltpu.VMEM((NZ, 128, LANES), F32),
        pltpu.VMEM((NX, 32, LANES), F32),
        pltpu.VMEM((NX, 32, LANES), BF16),
        pltpu.VMEM((NX, 32, LANES), BF16),
        pltpu.VMEM((NX, 32, LANES), F32),
        pltpu.VMEM((NX, 16, LANES), F32),
        pltpu.VMEM((NX, 16, LANES), F32),
        pltpu.VMEM((NZ, 8, LANES), F32),
        pltpu.VMEM((NZ, 8, LANES), F32),
        dma, dma, dma, dma((2,)),
        dma((2,)), dma((CH, 4)),
        dma((2,)), dma((2,)), dma((4,)),
        dma((6,)), dma((CH,)), dma((CH, 4)),
        dma, dma,
        dma, dma((CH,)),
        dma, dma((2, 2)), dma, dma((2,)),
        dma, dma, dma, dma,
    ]
    grad_hidden, grad_prob, grad_weight = pl.pallas_call(
        kernel,
        out_shape=(
            jax.ShapeDtypeStruct((pair, slots, units), BF16),
            jax.ShapeDtypeStruct((8, tok), F32),
            jax.ShapeDtypeStruct((256, pair * units), F32),
        ),
        in_specs=[anyspec, anyspec, anyspec, vm, vm, vm],
        out_specs=(anyspec, vm, anyspec),
        scratch_shapes=scratch,
        compiler_params=pltpu.CompilerParams(
            collective_id=0, has_side_effects=True, vmem_limit_bytes=67043328
        ),
        name="routed_backward",
    )(
        cotangent,
        hidden.reshape(pair, slots, units),
        down_weight,
        routes.T,
        gate_prob.T,
        sign_seed.reshape(16, 128),
    )
    return (
        grad_hidden.reshape(hidden.shape),
        grad_prob.T,
        grad_weight.reshape(256, pair, units),
    )


def solution(mesh):
    in_specs = (
        P(("dp", "expert"), None),
        P(("dp", "expert"), None),
        P(("dp", "expert"), None),
        P("dp", "expert", None, None, None),
        P("expert", None, None),
        P(),
    )
    out_specs = (
        P("dp", "expert", None, None, None),
        P(("dp", "expert"), None),
        P("dp", "expert", None),
    )
    return jax.shard_map(shards, mesh=mesh, in_specs=in_specs, out_specs=out_specs, check_vma=False)
```

```python
import functools
import math

import jax
import jax.numpy as jnp
from jax import lax
from jax.experimental import pallas as pl
from jax.experimental.pallas import tpu as pltpu
from jax.sharding import PartitionSpec as P

MESH = pl.DeviceIdType.MESH
BLOCK = 128
NX, NY, NZ = 4, 4, 8
CH = 8
LANES = 128
CW = 2 * LANES
MISS = -100.0
BF16, F32 = jnp.bfloat16, jnp.float32


def dot_nn(a, b):
    return lax.dot_general(a, b, (((1,), (0,)), ((), ())), preferred_element_type=F32)


def dot_nt(a, b):
    return lax.dot_general(a, b, (((1,), (1,)), ((), ())), preferred_element_type=F32)


def kernel(
    cot, hid_hbm, w_hbm, routes_t, gate_t, seed,
    gh_out, gp_out, gw_out,
    zbuf, sel, rg, xsend, relay, wbuf, hid, weighted_t, acc, gh_buf, gw_buf,
    part, part_in, y_relay, y_fin,
    table, t_rows, x_rows, x_out, d_in, d_tab,
    r_tab, r_mid, r_out, r_end,
    load_sem, w_sem, hid_sem, out_sem,
    zs_sem, z_recv, tz_sem, tz_half, tz_recv,
    xs_sem, x_recv, xrel_recv, tx_sem, tx_recv,
    p_send, p_recv, yr_send, yr_recv, yf_send, yf_recv,
    rx_send, rx_recv, rz_send, rz_recv,
):
    rows48 = 48
    dp = lax.axis_index("dp")
    ex = lax.axis_index("expert")
    y, core = dp // 2, lax.rem(dp, 2)
    x, z = ex // NZ, lax.rem(ex, NZ)
    up = lambda v, d, n: lax.rem(v + d, n)

    def x_dev(xx):
        return (dp, xx * NZ + z)

    def z_dev(zz):
        return (dp, x * NZ + zz)

    xr, xl = x_dev(up(x, 1, NX)), x_dev(up(x, NX - 1, NX))
    zr, zl = z_dev(up(z, 1, NZ)), z_dev(up(z, NZ - 1, NZ))
    yr, yl = (up(y, 1, NY) * 2 + core, ex), (up(y, NY - 1, NY) * 2 + core, ex)
    partner = (y * 2 + 1 - core, ex)

    def remote(src, dst, send, recv, dev):
        return pltpu.make_async_remote_copy(
            src_ref=src, dst_ref=dst, send_sem=send, recv_sem=recv,
            device_id=dev, device_id_type=MESH,
        )

    def wait_recv(dst, sem):
        remote(dst, dst, sem, sem, xr).wait_recv()

    def wait_send(src, sem):
        remote(src, src, sem, sem, xr).wait_send()

    barrier = pltpu.get_barrier_semaphore()
    peers = [zr, zl, yr, yl, partner]
    peers += [x_dev(up(x, d, NX)) for d in range(1, NX)]
    for peer in peers:
        pl.semaphore_signal(barrier, inc=1, device_id=peer, device_id_type=MESH)

    def base_of(c, k):
        return 512 * ((c + 2 * k) % NY) + 256 * k + LANES * (c // NY)

    for c in range(CH):
        for k in range(2):
            pltpu.make_async_copy(
                cot.at[:, pl.ds(base_of(c, k), LANES)],
                zbuf.at[c, z, :, pl.ds(LANES * k, LANES)], load_sem,
            ).start()
    pltpu.make_async_copy(hid_hbm, hid, hid_sem).start()
    for c in range(CH):
        for k in range(2):
            pltpu.make_async_copy(
                w_hbm.at[:, :, pl.ds(base_of(c, k), LANES)],
                wbuf.at[c, :, :, pl.ds(LANES * k, LANES)], w_sem,
            ).start()

    e_iota = lax.broadcasted_iota(jnp.int32, (64, LANES), 0)
    gates = gate_t[...].astype(F32)
    hit = jnp.zeros((64, LANES), F32)
    gate = jnp.zeros((64, LANES), F32)
    for k in range(8):
        eq = routes_t[k:k + 1, :] == e_iota
        hit = jnp.where(eq, 1.0, hit)
        gate = jnp.where(eq, gates[k:k + 1, :], gate)
    earlier = (
        lax.broadcasted_iota(jnp.int32, (LANES, LANES), 0)
        < lax.broadcasted_iota(jnp.int32, (LANES, LANES), 1)
    )
    rank = dot_nn(hit.astype(BF16), jnp.where(earlier, 1.0, 0.0).astype(BF16))
    table[z, 0:64, :] = jnp.where(hit > 0.5, rank, MISS).astype(BF16)
    table[z, 64:128, :] = gate.astype(BF16)
    pltpu.make_async_copy(zbuf.at[:, z], zbuf.at[:, z], load_sem).wait()
    pl.semaphore_wait(barrier, len(peers))

    lower, upper = pl.ds(0, 64), pl.ds(64, 64)

    def z_send(c, h):
        right, left = up(z, NZ - h, NZ), up(z, h, NZ)
        if h < 3:
            remote(zbuf.at[c, right], zbuf.at[c, right], zs_sem.at[0], z_recv.at[c, h], zr).start()
            remote(zbuf.at[c, left], zbuf.at[c, left], zs_sem.at[1], z_recv.at[c, h], zl).start()
        else:
            remote(zbuf.at[c, right, lower], zbuf.at[c, right, lower], zs_sem.at[0], z_recv.at[c, h], zr).start()
            remote(zbuf.at[c, left, upper], zbuf.at[c, left, upper], zs_sem.at[1], z_recv.at[c, h], zl).start()

    def z_wait(c, dist):
        wait_recv(zbuf.at[c, pl.ds(0, 2 if dist < 4 else 1)], z_recv.at[c, dist - 1])

    def z_relay(c, h):
        if h > 0:
            z_wait(c, h)
        z_send(c, h)

    def table_send(h):
        right, left = up(z, NZ - h, NZ), up(z, h, NZ)
        if h < 3:
            remote(table.at[right], table.at[right], tz_sem.at[0], tz_recv.at[h], zr).start()
            remote(table.at[left], table.at[left], tz_sem.at[1], tz_recv.at[h], zl).start()
        else:
            remote(table.at[right, lower], table.at[right, lower], tz_half.at[0], tz_recv.at[h], zr).start()
            remote(table.at[left, upper], table.at[left, upper], tz_half.at[1], tz_recv.at[h], zl).start()

    def table_rows(zs):
        block = table[zs].astype(F32)
        t_rows[zs] = block

    def table_wait(dist):
        wait_recv(table.at[pl.ds(0, 2 if dist < 4 else 1)], tz_recv.at[dist - 1])
        if dist < 4:
            table_send(dist)
            table_rows(up(z, NZ - dist, NZ))
        table_rows(up(z, dist, NZ))

    table_send(0)
    z_send(0, 0)
    z_send(1, 0)
    table_rows(z)

    r_iota = lax.broadcasted_iota(jnp.int32, (rows48, LANES), 0).astype(F32)

    def one_hot_pair(even_row, odd_row):
        return even_row == r_iota, odd_row + 24.0 == r_iota

    def build_sel(m):
        for dx in range(NX):
            xx = up(x, dx, NX)
            for j in range(2):
                row = pl.ds(16 * xx + 2 * z + j, 1)
                even, odd = one_hot_pair(t_rows[2 * m, row, :], t_rows[2 * m + 1, row, :])
                at = (dx * 2 + j) * rows48
                sel[m, at:at + rows48, 0:LANES] = jnp.where(even, 1.0, 0.0).astype(BF16)
                sel[m, at:at + rows48, LANES:2 * LANES] = jnp.where(odd, 1.0, 0.0).astype(BF16)

    def x_tables():
        for xx in range(NX):
            row = 16 * xx + 2 * z
            for zs in range(NZ):
                for j in range(2):
                    at = 2 * zs + j
                    x_rows[xx, at:at + 1, :] = t_rows[zs, pl.ds(row + j, 1), :]
                    x_rows[xx, 16 + at:17 + at, :] = t_rows[zs, pl.ds(64 + row + j, 1), :]
            x_out[xx] = x_rows[xx].astype(BF16)
        for d in range(1, NX):
            to = up(x, d, NX)
            remote(x_out.at[to], d_in.at[x], tx_sem, tx_recv, x_dev(to)).start()
        d_in[x] = x_out[x]

    step_sign = 2 * lax.rem(z, 2) - 1

    def pair_of(i):
        turn = jnp.where(i == 0, 0, jnp.where(i == 1, 4 + step_sign, jnp.where(i == 2, 4 - step_sign, 2)))
        return lax.rem(z // 2 + turn, 4)

    def step_of(s, t):
        if t < 0:
            s, t = s - 1, t + 8
        tail = s >= 1
        return (
            jnp.where(tail, 2 * s + t // 4, 2 * s + t % 2),
            jnp.where(tail, t % 4, t // 2),
        )

    def x_step(c, i):
        m = pair_of(i)
        tokens = zbuf[c, pl.ds(2 * m, 2)].reshape(2 * LANES, CW)
        rows = dot_nn(sel[m], tokens).astype(BF16)
        xsend[c, i] = rows[96:384].reshape(3, 2, rows48, CW)
        here = x * 4 + m
        remote(xsend.at[c, i, 1, 0], relay.at[c, i, 0], xs_sem.at[2], xrel_recv.at[c, i], xr).start()
        remote(xsend.at[c, i, 1, 1], relay.at[c, i, 1], xs_sem.at[3], xrel_recv.at[c, i], xl).start()
        remote(xsend.at[c, i, 0], rg.at[c, :, here], xs_sem.at[0], x_recv.at[c], xr).start()
        remote(xsend.at[c, i, 2], rg.at[c, :, here], xs_sem.at[1], x_recv.at[c], xl).start()
        rg[c, :, here] = rows[0:96].reshape(2, rows48, CW)

    def x_forward(c, i):
        m = pair_of(i)
        from_l, from_r = up(x, NX - 1, NX) * 4 + m, up(x, 1, NX) * 4 + m
        wait_recv(relay.at[c, i], xrel_recv.at[c, i])
        remote(relay.at[c, i, 0], rg.at[c, 0, from_l], xs_sem.at[4], x_recv.at[c], xr).start()
        remote(relay.at[c, i, 1], rg.at[c, 1, from_r], xs_sem.at[5], x_recv.at[c], xl).start()

    def x_wait(c):
        wait_recv(rg.at[c, :, pl.ds(0, 12)], x_recv.at[c])

    def pair_rows(p, j, row):
        xs, at = p // 4, 4 * lax.rem(p, 4) + j + row
        return d_tab[xs, pl.ds(at, 1), :], d_tab[xs, pl.ds(at + 2, 1), :]

    def slot_prob(p, j):
        even, odd = one_hot_pair(*pair_rows(p, j, 0))
        g_even, g_odd = pair_rows(p, j, 16)
        picked = jnp.where(even, g_even, 0.0) + jnp.where(odd, g_odd, 0.0)
        return jnp.sum(picked, axis=1, keepdims=True)

    def weigh():
        wait_recv(d_in.at[pl.ds(0, 3)], tx_recv)
        d_tab[...] = d_in[...].astype(F32)
        pltpu.make_async_copy(hid_hbm, hid, hid_sem).wait()

        def body(p, _):
            at = pl.ds(pl.multiple_of(p * rows48, 16), rows48)
            for j in range(2):
                rows = slot_prob(p, j) * hid[j, at, :].astype(F32)
                gh_buf[j, at, :] = rows.astype(BF16)
            return 0

        lax.fori_loop(0, 16, body, 0)
        for j in range(2):
            for q in range(6):
                cols = slice(LANES * q, LANES * (q + 1))
                weighted_t[j, cols, :] = gh_buf[j, :, cols].T

    def partial(c):
        for j in range(2):
            for q in range(3):
                fs = slice(256 * q, 256 * (q + 1))
                got = dot_nn(weighted_t[j, fs, :], rg[c, j].reshape(768, CW)).astype(BF16)
                for k in range(2):
                    part[c, k, j, fs, :] = got[:, LANES * k:LANES * (k + 1)]
            remote(part.at[c, 1 - core, j], part_in.at[c, j], p_send, p_recv.at[c], partner).start()

    def back(c):
        for j in range(2):
            for q in range(3):
                rs = slice(256 * q, 256 * (q + 1))
                acc[j, rs, :] += dot_nt(rg[c, j].reshape(768, CW)[rs], wbuf[c, j])

    def role(c):
        return up(y + NY, NY - lax.rem(c + 2 * core, NY), NY)

    def pair_add(c):
        half, at = c // NY, role(c)
        wait_recv(part_in.at[c], p_recv.at[c])
        for j in range(2):
            total = part[c, core, j].astype(F32) + part_in[c, j].astype(F32)
            part[c, core, j] = total.astype(BF16)
        mine = part.at[c, core]

        @pl.when(at == 2)
        def _():
            remote(mine.at[0], y_relay.at[half, 0], yr_send, yr_recv.at[half, 0], yr).start()
            remote(mine.at[1], y_relay.at[half, 1], yr_send, yr_recv.at[half, 1], yl).start()

        @pl.when(at == 3)
        def _():
            remote(mine.at[1], y_fin.at[half, 0, 1], yf_send, yf_recv.at[half], yr).start()

        @pl.when(at == 1)
        def _():
            remote(mine.at[0], y_fin.at[half, 1, 0], yf_send, yf_recv.at[half], yl).start()

    def relay_add(c):
        half, at = c // NY, role(c)
        for j, place, side, dev in ((0, 3, 0, yr), (1, 1, 1, yl)):
            @pl.when(at == place)
            def _(j=j, side=side, dev=dev):
                wait_recv(y_relay.at[half, j], yr_recv.at[half, j])
                total = part[c, core, j].astype(F32) + y_relay[half, j].astype(F32)
                part[c, core, j] = total.astype(BF16)
                remote(part.at[c, core, j], y_fin.at[half, side, j], yf_send, yf_recv.at[half], dev).start()

    def finish(c):
        half = c // NY

        @pl.when(role(c) == 0)
        def _():
            i0 = lax.broadcasted_iota(jnp.int32, (BLOCK, BLOCK), 0)
            i1 = lax.broadcasted_iota(jnp.int32, (BLOCK, BLOCK), 1)
            bits = i0 & i1
            bits = bits ^ (bits >> 4)
            bits = bits ^ (bits >> 2)
            bits = bits ^ (bits >> 1)
            sign = (2 * seed[pl.ds(4 * y + 2 * core + half, 1), :] - 1).astype(F32)
            turn = (jnp.where((bits & 1) == 1, -1.0, 1.0) * sign).astype(BF16)
            out_rows = pl.ds(pl.multiple_of(half * BLOCK, BLOCK), BLOCK)
            wait_recv(y_fin.at[half], yf_recv.at[half])
            for j in range(2):
                total = part[c, core, j].astype(F32) + y_fin[half, 0, j].astype(F32) + y_fin[half, 1, j].astype(F32)
                high = total.astype(BF16)
                low = (total - high.astype(F32)).astype(BF16)
                turned = (dot_nt(turn, high) + dot_nt(turn, low)) * (1.0 / math.sqrt(BLOCK))
                gw_buf[out_rows, 768 * j:768 * (j + 1)] = turned
            pltpu.make_async_copy(gw_buf.at[out_rows], gw_out.at[out_rows], out_sem.at[half]).start()

    acc[...] = jnp.zeros(acc.shape, F32)

    def double(s, _):
        first, more = s == 0, s > 0
        for t in range(8):
            q, h = t % 2, t // 2

            @pl.when(first)
            def _(q=q, h=h):
                z_wait(q, h + 1)
                if h < 3:
                    z_send(q, h + 1)
                if q == 0:
                    table_wait(h + 1)
                    build_sel(pair_of(h))

            if t in (0, 1, 2):
                @pl.when(more)
                def _(t=t):
                    if t == 0:
                        z_relay(2 * s + 1, 2)
                    else:
                        z_relay(2 * s + t - 1, 3)
            else:
                @pl.when(s < 3)
                def _(t=t):
                    z_relay(2 * s + 2 + (t - 3) % 2, (t - 3) // 2)

            c, i = step_of(s, t)
            if t in (3, 7):
                @pl.when(more)
                def _(c=c):
                    z_wait(c, 4)
            x_step(c, i)
            fc, fi = step_of(s, t - 3)
            if t < 3:
                @pl.when(more)
                def _(fc=fc, fi=fi):
                    x_forward(fc, fi)
            else:
                x_forward(fc, fi)

            at_one, later = s == 1, s > 1
            if t == 0:
                @pl.when(later)
                def _():
                    pair_add(2 * s - 3)
            if t == 2:
                @pl.when(at_one)
                def _():
                    weigh()

                @pl.when(later)
                def _():
                    x_wait(2 * s - 2)
                    partial(2 * s - 2)

                @pl.when(s == 2)
                def _():
                    relay_add(0)
            if t == 3:
                @pl.when(later)
                def _():
                    back(2 * s - 2)
                    relay_add(2 * s - 3)
            if t == 4:
                @pl.when(later)
                def _():
                    pair_add(2 * s - 2)
            if t == 5:
                @pl.when(at_one)
                def _():
                    pltpu.make_async_copy(wbuf, wbuf, w_sem).wait()
                    x_wait(0)
                    partial(0)
                    back(0)

                @pl.when(later)
                def _():
                    finish(jnp.where(s == 2, 0, 2))
            if t == 6:
                @pl.when(more)
                def _():
                    x_wait(2 * s - 1)
                    partial(2 * s - 1)
            if t == 7:
                @pl.when(first)
                def _():
                    x_tables()

                @pl.when(at_one)
                def _():
                    pair_add(0)

                @pl.when(more)
                def _():
                    back(2 * s - 1)

                @pl.when(later)
                def _():
                    relay_add(2 * s - 2)
                    finish(2 * s - 3)
        return 0

    lax.fori_loop(0, CH // 2, double, 0)

    x_forward(7, 1)
    x_forward(7, 2)
    pair_add(5)
    x_wait(6)
    partial(6)
    x_forward(7, 3)
    back(6)
    pair_add(6)
    relay_add(5)
    x_wait(7)
    partial(7)
    back(7)
    pair_add(7)
    relay_add(6)

    def outputs(p, _):
        at = pl.ds(pl.multiple_of(p * rows48, 16), rows48)
        xs, row = p // 4, 4 * lax.rem(p, 4)
        for j in range(2):
            rows = acc[j, at, :]
            gh_buf[j, at, :] = (slot_prob(p, j) * rows).astype(BF16)
            slot = jnp.sum(rows * hid[j, at, :].astype(F32), axis=1, keepdims=True)
            even, odd = one_hot_pair(*pair_rows(p, j, 0))
            r_tab[xs, pl.ds(row + j, 1), :] = jnp.sum(jnp.where(even, slot, 0.0), axis=0, keepdims=True)
            r_tab[xs, pl.ds(row + 2 + j, 1), :] = jnp.sum(jnp.where(odd, slot, 0.0), axis=0, keepdims=True)
        return 0

    lax.fori_loop(0, 8, outputs, 0)
    relay_add(7)
    lax.fori_loop(8, 16, outputs, 0)

    for d in range(1, NX):
        to = up(x, d, NX)
        remote(r_tab.at[to], r_mid.at[x], rx_send, rx_recv, x_dev(to)).start()
    r_mid[x] = r_tab[x]
    pltpu.make_async_copy(gh_buf, gh_out, hid_sem).start()
    finish(4)
    finish(5)
    wait_recv(r_mid.at[pl.ds(0, 3)], rx_recv)
    for zs in range(NZ):
        for xx in range(NX):
            r_out[zs, 2 * xx:2 * xx + 2, :] = r_mid[xx, 2 * zs:2 * zs + 2, :]
    for d in range(1, NZ):
        to = up(z, d, NZ)
        remote(r_out.at[to], r_end.at[z], rz_send, rz_recv, z_dev(to)).start()
    r_end[z] = r_out[z]
    finish(6)
    finish(7)
    wait_recv(r_end.at[pl.ds(0, 7)], rz_recv)
    grad_prob = jnp.zeros((8, LANES), F32)
    chosen = routes_t[...]
    for zz in range(NZ):
        for xx in range(NX):
            for j in range(2):
                e = 16 * xx + 2 * zz + j
                row = 2 * xx + j
                grad_prob = jnp.where(chosen == e, r_end[zz, row:row + 1, :], grad_prob)
    gp_out[...] = grad_prob

    wait_send(zbuf.at[pl.ds(0, 4), pl.ds(0, 7)], zs_sem.at[0])
    wait_send(zbuf.at[pl.ds(0, 4), pl.ds(0, 7)], zs_sem.at[1])
    for side in range(2):
        wait_send(table.at[pl.ds(0, 3)], tz_sem.at[side])
        wait_send(table.at[0, lower], tz_half.at[side])
        wait_send(xsend.at[:, :, 2 * side], xs_sem.at[side])
        wait_send(xsend.at[:, :, 1, side], xs_sem.at[2 + side])
        wait_send(relay.at[:, :, side], xs_sem.at[4 + side])
    wait_send(x_out.at[pl.ds(0, 3)], tx_sem)
    wait_send(r_tab.at[pl.ds(0, 3)], rx_send)
    wait_send(r_out.at[pl.ds(0, 7)], rz_send)
    wait_send(part.at[:, 0], p_send)
    wait_send(part.at[pl.ds(0, 2), 0], yr_send)
    wait_send(part.at[pl.ds(0, 4), 0], yf_send)
    pltpu.make_async_copy(gh_buf, gh_out, hid_sem).wait()
    for half in range(2):
        out_rows = pl.ds(BLOCK * half, BLOCK)
        pltpu.make_async_copy(gw_buf.at[out_rows], gw_out.at[out_rows], out_sem.at[half]).wait()


def shards(cotangent, gate_prob, routes, hidden, down_weight, sign_seed):
    tok, features = cotangent.shape
    _, pair, sources, cap, units = hidden.shape
    slots = sources * cap
    vm = pl.BlockSpec(memory_space=pltpu.VMEM)
    anyspec = pl.BlockSpec(memory_space=pl.ANY)
    dma = pltpu.SemaphoreType.DMA
    scratch = [
        pltpu.VMEM((CH, NZ, tok, CW), BF16),
        pltpu.VMEM((4, 384, 256), BF16),
        pltpu.VMEM((CH, 2, 16, 48, CW), BF16),
        pltpu.VMEM((CH, 4, 3, 2, 48, CW), BF16),
        pltpu.VMEM((CH, 4, 2, 48, CW), BF16),
        pltpu.VMEM((CH, 2, units, CW), BF16),
        pltpu.VMEM((2, slots, units), BF16),
        pltpu.VMEM((2, units, slots), BF16),
        pltpu.VMEM((2, slots, units), F32),
        pltpu.VMEM((2, slots, units), BF16),
        pltpu.VMEM((256, pair * units), F32),
        pltpu.VMEM((CH, 2, 2, units, LANES), BF16),
        pltpu.VMEM((CH, 2, units, LANES), BF16),
        pltpu.VMEM((2, 2, units, LANES), BF16),
        pltpu.VMEM((2, 2, 2, units, LANES), BF16),
        pltpu.VMEM((NZ, 128, LANES), BF16),
        pltpu.VMEM((NZ, 128, LANES), F32),
        pltpu.VMEM((NX, 32, LANES), F32),
        pltpu.VMEM((NX, 32, LANES), BF16),
        pltpu.VMEM((NX, 32, LANES), BF16),
        pltpu.VMEM((NX, 32, LANES), F32),
        pltpu.VMEM((NX, 16, LANES), F32),
        pltpu.VMEM((NX, 16, LANES), F32),
        pltpu.VMEM((NZ, 8, LANES), F32),
        pltpu.VMEM((NZ, 8, LANES), F32),
        dma, dma, dma, dma((2,)),
        dma((2,)), dma((CH, 4)),
        dma((2,)), dma((2,)), dma((4,)),
        dma((6,)), dma((CH,)), dma((CH, 4)),
        dma, dma,
        dma, dma((CH,)),
        dma, dma((2, 2)), dma, dma((2,)),
        dma, dma, dma, dma,
    ]
    grad_hidden, grad_prob, grad_weight = pl.pallas_call(
        kernel,
        out_shape=(
            jax.ShapeDtypeStruct((pair, slots, units), BF16),
            jax.ShapeDtypeStruct((8, tok), F32),
            jax.ShapeDtypeStruct((256, pair * units), F32),
        ),
        in_specs=[anyspec, anyspec, anyspec, vm, vm, vm],
        out_specs=(anyspec, vm, anyspec),
        scratch_shapes=scratch,
        compiler_params=pltpu.CompilerParams(
            collective_id=0, has_side_effects=True, vmem_limit_bytes=67043328
        ),
        name="routed_backward",
    )(
        cotangent,
        hidden.reshape(pair, slots, units),
        down_weight,
        routes.T,
        gate_prob.T,
        sign_seed.reshape(16, 128),
    )
    return (
        grad_hidden.reshape(hidden.shape),
        grad_prob.T,
        grad_weight.reshape(256, pair, units),
    )


def solution(mesh):
    in_specs = (
        P(("dp", "expert"), None),
        P(("dp", "expert"), None),
        P(("dp", "expert"), None),
        P("dp", "expert", None, None, None),
        P("expert", None, None),
        P(),
    )
    out_specs = (
        P("dp", "expert", None, None, None),
        P(("dp", "expert"), None),
        P("dp", "expert", None),
    )
    return jax.shard_map(shards, mesh=mesh, in_specs=in_specs, out_specs=out_specs, check_vma=False)
```

```python
import functools
import math

import jax
import jax.numpy as jnp
from jax import lax
from jax.experimental import pallas as pl
from jax.experimental.pallas import tpu as pltpu
from jax.sharding import PartitionSpec as P

MESH = pl.DeviceIdType.MESH
BLOCK = 128
NX, NY, NZ = 4, 4, 8
CH = 8
LANES = 128
CW = 2 * LANES
MISS = -100.0
BF16, F32 = jnp.bfloat16, jnp.float32


def dot_nn(a, b):
    return lax.dot_general(a, b, (((1,), (0,)), ((), ())), preferred_element_type=F32)


def dot_nt(a, b):
    return lax.dot_general(a, b, (((1,), (1,)), ((), ())), preferred_element_type=F32)


def kernel(
    cot, hid_hbm, w_hbm, routes_t, gate_t, seed,
    gh_out, gp_out, gw_out,
    zbuf, sel, rg, xsend, relay, wbuf, hid, weighted_t, acc, gh_buf, gw_buf,
    part, part_in, y_relay, y_fin,
    table, t_rows, x_rows, x_out, d_in, d_tab,
    r_tab, r_mid, r_out, r_end,
    load_sem, w_sem, hid_sem, out_sem,
    zs_sem, z_recv, tz_sem, tz_half, tz_recv,
    xs_sem, x_recv, xrel_recv, tx_sem, tx_recv,
    p_send, p_recv, yr_send, yr_recv, yf_send, yf_recv,
    rx_send, rx_recv, rz_send, rz_recv,
):
    rows48 = 48
    dp = lax.axis_index("dp")
    ex = lax.axis_index("expert")
    y, core = dp // 2, lax.rem(dp, 2)
    x, z = ex // NZ, lax.rem(ex, NZ)
    up = lambda v, d, n: lax.rem(v + d, n)

    def x_dev(xx):
        return (dp, xx * NZ + z)

    def z_dev(zz):
        return (dp, x * NZ + zz)

    xr, xl = x_dev(up(x, 1, NX)), x_dev(up(x, NX - 1, NX))
    zr, zl = z_dev(up(z, 1, NZ)), z_dev(up(z, NZ - 1, NZ))
    yr, yl = (up(y, 1, NY) * 2 + core, ex), (up(y, NY - 1, NY) * 2 + core, ex)
    partner = (y * 2 + 1 - core, ex)

    def remote(src, dst, send, recv, dev):
        return pltpu.make_async_remote_copy(
            src_ref=src, dst_ref=dst, send_sem=send, recv_sem=recv,
            device_id=dev, device_id_type=MESH,
        )

    def wait_recv(dst, sem):
        remote(dst, dst, sem, sem, xr).wait_recv()

    def wait_send(src, sem):
        remote(src, src, sem, sem, xr).wait_send()

    barrier = pltpu.get_barrier_semaphore()
    peers = [zr, zl, yr, yl, partner]
    peers += [x_dev(up(x, d, NX)) for d in range(1, NX)]
    for peer in peers:
        pl.semaphore_signal(barrier, inc=1, device_id=peer, device_id_type=MESH)

    def base_of(c, k):
        return 512 * ((c + 2 * k) % NY) + 256 * k + LANES * (c // NY)

    for c in range(CH):
        for k in range(2):
            pltpu.make_async_copy(
                cot.at[:, pl.ds(base_of(c, k), LANES)],
                zbuf.at[c, z, :, pl.ds(LANES * k, LANES)], load_sem,
            ).start()
    pltpu.make_async_copy(hid_hbm, hid, hid_sem).start()
    for c in range(CH):
        for k in range(2):
            pltpu.make_async_copy(
                w_hbm.at[:, :, pl.ds(base_of(c, k), LANES)],
                wbuf.at[c, :, :, pl.ds(LANES * k, LANES)], w_sem,
            ).start()

    e_iota = lax.broadcasted_iota(jnp.int32, (64, LANES), 0)
    gates = gate_t[...].astype(F32)
    hit = jnp.zeros((64, LANES), F32)
    gate = jnp.zeros((64, LANES), F32)
    for k in range(8):
        eq = routes_t[k:k + 1, :] == e_iota
        hit = jnp.where(eq, 1.0, hit)
        gate = jnp.where(eq, gates[k:k + 1, :], gate)
    earlier = (
        lax.broadcasted_iota(jnp.int32, (LANES, LANES), 0)
        < lax.broadcasted_iota(jnp.int32, (LANES, LANES), 1)
    )
    rank = dot_nn(hit.astype(BF16), jnp.where(earlier, 1.0, 0.0).astype(BF16))
    table[z, 0:64, :] = jnp.where(hit > 0.5, rank, MISS).astype(BF16)
    table[z, 64:128, :] = gate.astype(BF16)
    pltpu.make_async_copy(zbuf.at[:, z], zbuf.at[:, z], load_sem).wait()
    pl.semaphore_wait(barrier, len(peers))

    lower, upper = pl.ds(0, 64), pl.ds(64, 64)

    def z_send(c, h):
        right, left = up(z, NZ - h, NZ), up(z, h, NZ)
        if h < 3:
            remote(zbuf.at[c, right], zbuf.at[c, right], zs_sem.at[0], z_recv.at[c, h], zr).start()
            remote(zbuf.at[c, left], zbuf.at[c, left], zs_sem.at[1], z_recv.at[c, h], zl).start()
        else:
            remote(zbuf.at[c, right, lower], zbuf.at[c, right, lower], zs_sem.at[0], z_recv.at[c, h], zr).start()
            remote(zbuf.at[c, left, upper], zbuf.at[c, left, upper], zs_sem.at[1], z_recv.at[c, h], zl).start()

    def z_wait(c, dist):
        wait_recv(zbuf.at[c, pl.ds(0, 2 if dist < 4 else 1)], z_recv.at[c, dist - 1])

    def z_relay(c, h):
        if h > 0:
            z_wait(c, h)
        z_send(c, h)

    def table_send(h):
        right, left = up(z, NZ - h, NZ), up(z, h, NZ)
        if h < 3:
            remote(table.at[right], table.at[right], tz_sem.at[0], tz_recv.at[h], zr).start()
            remote(table.at[left], table.at[left], tz_sem.at[1], tz_recv.at[h], zl).start()
        else:
            remote(table.at[right, lower], table.at[right, lower], tz_half.at[0], tz_recv.at[h], zr).start()
            remote(table.at[left, upper], table.at[left, upper], tz_half.at[1], tz_recv.at[h], zl).start()

    def table_rows(zs):
        block = table[zs].astype(F32)
        t_rows[zs] = block

    def table_wait(dist):
        wait_recv(table.at[pl.ds(0, 2 if dist < 4 else 1)], tz_recv.at[dist - 1])
        if dist < 4:
            table_send(dist)
            table_rows(up(z, NZ - dist, NZ))
        table_rows(up(z, dist, NZ))

    table_send(0)
    z_send(0, 0)
    z_send(1, 0)
    table_rows(z)

    r_iota = lax.broadcasted_iota(jnp.int32, (rows48, LANES), 0).astype(F32)

    def one_hot_pair(even_row, odd_row):
        return even_row == r_iota, odd_row + 24.0 == r_iota

    def build_sel(m):
        for dx in range(NX):
            xx = up(x, dx, NX)
            for j in range(2):
                row = pl.ds(16 * xx + 2 * z + j, 1)
                even, odd = one_hot_pair(t_rows[2 * m, row, :], t_rows[2 * m + 1, row, :])
                at = (dx * 2 + j) * rows48
                sel[m, at:at + rows48, 0:LANES] = jnp.where(even, 1.0, 0.0).astype(BF16)
                sel[m, at:at + rows48, LANES:2 * LANES] = jnp.where(odd, 1.0, 0.0).astype(BF16)

    def x_tables():
        for xx in range(NX):
            row = 16 * xx + 2 * z
            for zs in range(NZ):
                for j in range(2):
                    at = 2 * zs + j
                    x_rows[xx, at:at + 1, :] = t_rows[zs, pl.ds(row + j, 1), :]
                    x_rows[xx, 16 + at:17 + at, :] = t_rows[zs, pl.ds(64 + row + j, 1), :]
            x_out[xx] = x_rows[xx].astype(BF16)
        for d in range(1, NX):
            to = up(x, d, NX)
            remote(x_out.at[to], d_in.at[x], tx_sem, tx_recv, x_dev(to)).start()
        d_in[x] = x_out[x]

    step_sign = 2 * lax.rem(z, 2) - 1

    def pair_of(i):
        turn = jnp.where(i == 0, 0, jnp.where(i == 1, 4 + step_sign, jnp.where(i == 2, 4 - step_sign, 2)))
        return lax.rem(z // 2 + turn, 4)

    def step_of(s, t):
        if t < 0:
            s, t = s - 1, t + 8
        tail = s >= 1
        return (
            jnp.where(tail, 2 * s + t // 4, 2 * s + t % 2),
            jnp.where(tail, t % 4, t // 2),
        )

    def x_step(c, i):
        m = pair_of(i)
        tokens = zbuf[c, pl.ds(2 * m, 2)].reshape(2 * LANES, CW)
        rows = dot_nn(sel[m], tokens).astype(BF16)
        xsend[c, i] = rows[96:384].reshape(3, 2, rows48, CW)
        here = x * 4 + m
        remote(xsend.at[c, i, 1, 0], relay.at[c, i, 0], xs_sem.at[2], xrel_recv.at[c, i], xr).start()
        remote(xsend.at[c, i, 1, 1], relay.at[c, i, 1], xs_sem.at[3], xrel_recv.at[c, i], xl).start()
        remote(xsend.at[c, i, 0], rg.at[c, :, here], xs_sem.at[0], x_recv.at[c], xr).start()
        remote(xsend.at[c, i, 2], rg.at[c, :, here], xs_sem.at[1], x_recv.at[c], xl).start()
        rg[c, :, here] = rows[0:96].reshape(2, rows48, CW)

    def x_forward(c, i):
        m = pair_of(i)
        from_l, from_r = up(x, NX - 1, NX) * 4 + m, up(x, 1, NX) * 4 + m
        wait_recv(relay.at[c, i], xrel_recv.at[c, i])
        remote(relay.at[c, i, 0], rg.at[c, 0, from_l], xs_sem.at[4], x_recv.at[c], xr).start()
        remote(relay.at[c, i, 1], rg.at[c, 1, from_r], xs_sem.at[5], x_recv.at[c], xl).start()

    def x_wait(c):
        wait_recv(rg.at[c, :, pl.ds(0, 12)], x_recv.at[c])

    def pair_rows(p, j, row):
        xs, at = p // 4, 4 * lax.rem(p, 4) + j + row
        return d_tab[xs, pl.ds(at, 1), :], d_tab[xs, pl.ds(at + 2, 1), :]

    def slot_prob(p, j):
        even, odd = one_hot_pair(*pair_rows(p, j, 0))
        g_even, g_odd = pair_rows(p, j, 16)
        picked = jnp.where(even, g_even, 0.0) + jnp.where(odd, g_odd, 0.0)
        return jnp.sum(picked, axis=1, keepdims=True)

    def weigh():
        wait_recv(d_in.at[pl.ds(0, 3)], tx_recv)
        d_tab[...] = d_in[...].astype(F32)
        pltpu.make_async_copy(hid_hbm, hid, hid_sem).wait()

        def body(p, _):
            at = pl.ds(pl.multiple_of(p * rows48, 16), rows48)
            for j in range(2):
                rows = slot_prob(p, j) * hid[j, at, :].astype(F32)
                gh_buf[j, at, :] = rows.astype(BF16)
            return 0

        lax.fori_loop(0, 16, body, 0)
        for j in range(2):
            for q in range(6):
                cols = slice(LANES * q, LANES * (q + 1))
                weighted_t[j, cols, :] = gh_buf[j, :, cols].T

    def partial(c):
        for j in range(2):
            for q in range(3):
                fs = slice(256 * q, 256 * (q + 1))
                got = dot_nn(weighted_t[j, fs, :], rg[c, j].reshape(768, CW)).astype(BF16)
                for k in range(2):
                    part[c, k, j, fs, :] = got[:, LANES * k:LANES * (k + 1)]
            remote(part.at[c, 1 - core, j], part_in.at[c, j], p_send, p_recv.at[c], partner).start()

    def back(c):
        for j in range(2):
            for q in range(3):
                rs = slice(256 * q, 256 * (q + 1))
                acc[j, rs, :] += dot_nt(rg[c, j].reshape(768, CW)[rs], wbuf[c, j])

    def role(c):
        return up(y + NY, NY - lax.rem(c + 2 * core, NY), NY)

    def pair_add(c):
        half, at = c // NY, role(c)
        wait_recv(part_in.at[c], p_recv.at[c])
        for j in range(2):
            total = part[c, core, j].astype(F32) + part_in[c, j].astype(F32)
            part[c, core, j] = total.astype(BF16)
        mine = part.at[c, core]

        @pl.when(at == 2)
        def _():
            remote(mine.at[0], y_relay.at[half, 0], yr_send, yr_recv.at[half, 0], yr).start()
            remote(mine.at[1], y_relay.at[half, 1], yr_send, yr_recv.at[half, 1], yl).start()

        @pl.when(at == 3)
        def _():
            remote(mine.at[1], y_fin.at[half, 0, 1], yf_send, yf_recv.at[half], yr).start()

        @pl.when(at == 1)
        def _():
            remote(mine.at[0], y_fin.at[half, 1, 0], yf_send, yf_recv.at[half], yl).start()

    def relay_add(c):
        half, at = c // NY, role(c)
        for j, place, side, dev in ((0, 3, 0, yr), (1, 1, 1, yl)):
            @pl.when(at == place)
            def _(j=j, side=side, dev=dev):
                wait_recv(y_relay.at[half, j], yr_recv.at[half, j])
                total = part[c, core, j].astype(F32) + y_relay[half, j].astype(F32)
                part[c, core, j] = total.astype(BF16)
                remote(part.at[c, core, j], y_fin.at[half, side, j], yf_send, yf_recv.at[half], dev).start()

    def finish(c):
        half = c // NY

        @pl.when(role(c) == 0)
        def _():
            i0 = lax.broadcasted_iota(jnp.int32, (BLOCK, BLOCK), 0)
            i1 = lax.broadcasted_iota(jnp.int32, (BLOCK, BLOCK), 1)
            bits = i0 & i1
            bits = bits ^ (bits >> 4)
            bits = bits ^ (bits >> 2)
            bits = bits ^ (bits >> 1)
            sign = (2 * seed[pl.ds(4 * y + 2 * core + half, 1), :] - 1).astype(F32)
            turn = (jnp.where((bits & 1) == 1, -1.0, 1.0) * sign).astype(BF16)
            out_rows = pl.ds(pl.multiple_of(half * BLOCK, BLOCK), BLOCK)
            wait_recv(y_fin.at[half], yf_recv.at[half])
            for j in range(2):
                total = part[c, core, j].astype(F32) + y_fin[half, 0, j].astype(F32) + y_fin[half, 1, j].astype(F32)
                high = total.astype(BF16)
                low = (total - high.astype(F32)).astype(BF16)
                turned = (dot_nt(turn, high) + dot_nt(turn, low)) * (1.0 / math.sqrt(BLOCK))
                gw_buf[out_rows, 768 * j:768 * (j + 1)] = turned
            pltpu.make_async_copy(gw_buf.at[out_rows], gw_out.at[out_rows], out_sem.at[half]).start()

    acc[...] = jnp.zeros(acc.shape, F32)

    def double(s, _):
        first, more = s == 0, s > 0
        for t in range(8):
            q, h = t % 2, t // 2

            @pl.when(first)
            def _(q=q, h=h):
                z_wait(q, h + 1)
                if h < 3:
                    z_send(q, h + 1)
                if q == 0:
                    table_wait(h + 1)
                    build_sel(pair_of(h))

            if t in (0, 1, 2):
                @pl.when(more)
                def _(t=t):
                    if t == 0:
                        z_relay(2 * s + 1, 2)
                    else:
                        z_relay(2 * s + t - 1, 3)
            else:
                @pl.when(s < 3)
                def _(t=t):
                    z_relay(2 * s + 2 + (t - 3) % 2, (t - 3) // 2)

            c, i = step_of(s, t)
            if t in (3, 7):
                @pl.when(more)
                def _(c=c):
                    z_wait(c, 4)
            x_step(c, i)
            fc, fi = step_of(s, t - 3)
            if t < 3:
                @pl.when(more)
                def _(fc=fc, fi=fi):
                    x_forward(fc, fi)
            else:
                x_forward(fc, fi)

            at_one, later = s == 1, s > 1
            if t == 0:
                @pl.when(later)
                def _():
                    pair_add(2 * s - 3)
            if t == 2:
                @pl.when(at_one)
                def _():
                    weigh()

                @pl.when(later)
                def _():
                    x_wait(2 * s - 2)
                    partial(2 * s - 2)

                @pl.when(s == 2)
                def _():
                    relay_add(0)
            if t == 3:
                @pl.when(later)
                def _():
                    back(2 * s - 2)
                    relay_add(2 * s - 3)
            if t == 4:
                @pl.when(later)
                def _():
                    pair_add(2 * s - 2)
            if t == 5:
                @pl.when(at_one)
                def _():
                    pltpu.make_async_copy(wbuf, wbuf, w_sem).wait()
                    x_wait(0)
                    partial(0)
                    back(0)

                @pl.when(later)
                def _():
                    finish(jnp.where(s == 2, 0, 2))
            if t == 6:
                @pl.when(more)
                def _():
                    x_wait(2 * s - 1)
                    partial(2 * s - 1)
            if t == 7:
                @pl.when(first)
                def _():
                    x_tables()

                @pl.when(at_one)
                def _():
                    pair_add(0)

                @pl.when(more)
                def _():
                    back(2 * s - 1)

                @pl.when(later)
                def _():
                    relay_add(2 * s - 2)
                    finish(2 * s - 3)
        return 0

    lax.fori_loop(0, CH // 2, double, 0)

    x_forward(7, 1)
    x_forward(7, 2)
    pair_add(5)
    x_wait(6)
    partial(6)
    x_forward(7, 3)
    back(6)
    x_wait(7)
    partial(7)
    pair_add(6)
    relay_add(5)
    back(7)
    pair_add(7)
    relay_add(6)

    def outputs(p, _):
        at = pl.ds(pl.multiple_of(p * rows48, 16), rows48)
        xs, row = p // 4, 4 * lax.rem(p, 4)
        for j in range(2):
            rows = acc[j, at, :]
            gh_buf[j, at, :] = (slot_prob(p, j) * rows).astype(BF16)
            slot = jnp.sum(rows * hid[j, at, :].astype(F32), axis=1, keepdims=True)
            even, odd = one_hot_pair(*pair_rows(p, j, 0))
            r_tab[xs, pl.ds(row + j, 1), :] = jnp.sum(jnp.where(even, slot, 0.0), axis=0, keepdims=True)
            r_tab[xs, pl.ds(row + 2 + j, 1), :] = jnp.sum(jnp.where(odd, slot, 0.0), axis=0, keepdims=True)
        return 0

    lax.fori_loop(0, 8, outputs, 0)
    relay_add(7)
    lax.fori_loop(8, 16, outputs, 0)

    for d in range(1, NX):
        to = up(x, d, NX)
        remote(r_tab.at[to], r_mid.at[x], rx_send, rx_recv, x_dev(to)).start()
    r_mid[x] = r_tab[x]
    pltpu.make_async_copy(gh_buf, gh_out, hid_sem).start()
    finish(4)
    finish(5)
    wait_recv(r_mid.at[pl.ds(0, 3)], rx_recv)
    for zs in range(NZ):
        for xx in range(NX):
            r_out[zs, 2 * xx:2 * xx + 2, :] = r_mid[xx, 2 * zs:2 * zs + 2, :]
    for d in range(1, NZ):
        to = up(z, d, NZ)
        remote(r_out.at[to], r_end.at[z], rz_send, rz_recv, z_dev(to)).start()
    r_end[z] = r_out[z]
    finish(6)
    finish(7)
    wait_recv(r_end.at[pl.ds(0, 7)], rz_recv)
    grad_prob = jnp.zeros((8, LANES), F32)
    chosen = routes_t[...]
    for zz in range(NZ):
        for xx in range(NX):
            for j in range(2):
                e = 16 * xx + 2 * zz + j
                row = 2 * xx + j
                grad_prob = jnp.where(chosen == e, r_end[zz, row:row + 1, :], grad_prob)
    gp_out[...] = grad_prob

    wait_send(zbuf.at[pl.ds(0, 4), pl.ds(0, 7)], zs_sem.at[0])
    wait_send(zbuf.at[pl.ds(0, 4), pl.ds(0, 7)], zs_sem.at[1])
    for side in range(2):
        wait_send(table.at[pl.ds(0, 3)], tz_sem.at[side])
        wait_send(table.at[0, lower], tz_half.at[side])
        wait_send(xsend.at[:, :, 2 * side], xs_sem.at[side])
        wait_send(xsend.at[:, :, 1, side], xs_sem.at[2 + side])
        wait_send(relay.at[:, :, side], xs_sem.at[4 + side])
    wait_send(x_out.at[pl.ds(0, 3)], tx_sem)
    wait_send(r_tab.at[pl.ds(0, 3)], rx_send)
    wait_send(r_out.at[pl.ds(0, 7)], rz_send)
    wait_send(part.at[:, 0], p_send)
    wait_send(part.at[pl.ds(0, 2), 0], yr_send)
    wait_send(part.at[pl.ds(0, 4), 0], yf_send)
    pltpu.make_async_copy(gh_buf, gh_out, hid_sem).wait()
    for half in range(2):
        out_rows = pl.ds(BLOCK * half, BLOCK)
        pltpu.make_async_copy(gw_buf.at[out_rows], gw_out.at[out_rows], out_sem.at[half]).wait()


def shards(cotangent, gate_prob, routes, hidden, down_weight, sign_seed):
    tok, features = cotangent.shape
    _, pair, sources, cap, units = hidden.shape
    slots = sources * cap
    vm = pl.BlockSpec(memory_space=pltpu.VMEM)
    anyspec = pl.BlockSpec(memory_space=pl.ANY)
    dma = pltpu.SemaphoreType.DMA
    scratch = [
        pltpu.VMEM((CH, NZ, tok, CW), BF16),
        pltpu.VMEM((4, 384, 256), BF16),
        pltpu.VMEM((CH, 2, 16, 48, CW), BF16),
        pltpu.VMEM((CH, 4, 3, 2, 48, CW), BF16),
        pltpu.VMEM((CH, 4, 2, 48, CW), BF16),
        pltpu.VMEM((CH, 2, units, CW), BF16),
        pltpu.VMEM((2, slots, units), BF16),
        pltpu.VMEM((2, units, slots), BF16),
        pltpu.VMEM((2, slots, units), F32),
        pltpu.VMEM((2, slots, units), BF16),
        pltpu.VMEM((256, pair * units), F32),
        pltpu.VMEM((CH, 2, 2, units, LANES), BF16),
        pltpu.VMEM((CH, 2, units, LANES), BF16),
        pltpu.VMEM((2, 2, units, LANES), BF16),
        pltpu.VMEM((2, 2, 2, units, LANES), BF16),
        pltpu.VMEM((NZ, 128, LANES), BF16),
        pltpu.VMEM((NZ, 128, LANES), F32),
        pltpu.VMEM((NX, 32, LANES), F32),
        pltpu.VMEM((NX, 32, LANES), BF16),
        pltpu.VMEM((NX, 32, LANES), BF16),
        pltpu.VMEM((NX, 32, LANES), F32),
        pltpu.VMEM((NX, 16, LANES), F32),
        pltpu.VMEM((NX, 16, LANES), F32),
        pltpu.VMEM((NZ, 8, LANES), F32),
        pltpu.VMEM((NZ, 8, LANES), F32),
        dma, dma, dma, dma((2,)),
        dma((2,)), dma((CH, 4)),
        dma((2,)), dma((2,)), dma((4,)),
        dma((6,)), dma((CH,)), dma((CH, 4)),
        dma, dma,
        dma, dma((CH,)),
        dma, dma((2, 2)), dma, dma((2,)),
        dma, dma, dma, dma,
    ]
    grad_hidden, grad_prob, grad_weight = pl.pallas_call(
        kernel,
        out_shape=(
            jax.ShapeDtypeStruct((pair, slots, units), BF16),
            jax.ShapeDtypeStruct((8, tok), F32),
            jax.ShapeDtypeStruct((256, pair * units), F32),
        ),
        in_specs=[anyspec, anyspec, anyspec, vm, vm, vm],
        out_specs=(anyspec, vm, anyspec),
        scratch_shapes=scratch,
        compiler_params=pltpu.CompilerParams(
            collective_id=0, has_side_effects=True, vmem_limit_bytes=67043328
        ),
        name="routed_backward",
    )(
        cotangent,
        hidden.reshape(pair, slots, units),
        down_weight,
        routes.T,
        gate_prob.T,
        sign_seed.reshape(16, 128),
    )
    return (
        grad_hidden.reshape(hidden.shape),
        grad_prob.T,
        grad_weight.reshape(256, pair, units),
    )


def solution(mesh):
    in_specs = (
        P(("dp", "expert"), None),
        P(("dp", "expert"), None),
        P(("dp", "expert"), None),
        P("dp", "expert", None, None, None),
        P("expert", None, None),
        P(),
    )
    out_specs = (
        P("dp", "expert", None, None, None),
        P(("dp", "expert"), None),
        P("dp", "expert", None),
    )
    return jax.shard_map(shards, mesh=mesh, in_specs=in_specs, out_specs=out_specs, check_vma=False)
```

```python
import functools
import math

import jax
import jax.numpy as jnp
from jax import lax
from jax.experimental import pallas as pl
from jax.experimental.pallas import tpu as pltpu
from jax.sharding import PartitionSpec as P

MESH = pl.DeviceIdType.MESH
BLOCK = 128
NX, NY, NZ = 4, 4, 8
CH = 8
LANES = 128
CW = 2 * LANES
MISS = -100.0
BF16, F32 = jnp.bfloat16, jnp.float32


def dot_nn(a, b):
    return lax.dot_general(a, b, (((1,), (0,)), ((), ())), preferred_element_type=F32)


def dot_nt(a, b):
    return lax.dot_general(a, b, (((1,), (1,)), ((), ())), preferred_element_type=F32)


def kernel(
    cot, hid_hbm, w_hbm, routes_t, gate_t, seed,
    gh_out, gp_out, gw_out,
    zbuf, sel, rg, xsend, relay, wbuf, hid, weighted_t, acc, gh_buf, gw_buf,
    part, part_in, y_relay, y_fin,
    table, t_rows, x_rows, x_out, d_in, d_tab,
    r_tab, r_mid, r_out, r_end,
    load_sem, w_sem, hid_sem, out_sem,
    zs_sem, z_recv, tz_sem, tz_half, tz_recv,
    xs_sem, x_recv, xrel_recv, tx_sem, tx_recv,
    p_send, p_recv, yr_send, yr_recv, yf_send, yf_recv,
    rx_send, rx_recv, rz_send, rz_recv,
):
    rows48 = 48
    dp = lax.axis_index("dp")
    ex = lax.axis_index("expert")
    y, core = dp // 2, lax.rem(dp, 2)
    x, z = ex // NZ, lax.rem(ex, NZ)
    up = lambda v, d, n: lax.rem(v + d, n)

    def x_dev(xx):
        return (dp, xx * NZ + z)

    def z_dev(zz):
        return (dp, x * NZ + zz)

    xr, xl = x_dev(up(x, 1, NX)), x_dev(up(x, NX - 1, NX))
    zr, zl = z_dev(up(z, 1, NZ)), z_dev(up(z, NZ - 1, NZ))
    yr, yl = (up(y, 1, NY) * 2 + core, ex), (up(y, NY - 1, NY) * 2 + core, ex)
    partner = (y * 2 + 1 - core, ex)

    def remote(src, dst, send, recv, dev):
        return pltpu.make_async_remote_copy(
            src_ref=src, dst_ref=dst, send_sem=send, recv_sem=recv,
            device_id=dev, device_id_type=MESH,
        )

    def wait_recv(dst, sem):
        remote(dst, dst, sem, sem, xr).wait_recv()

    def wait_send(src, sem):
        remote(src, src, sem, sem, xr).wait_send()

    barrier = pltpu.get_barrier_semaphore()
    peers = [zr, zl, yr, yl, partner]
    peers += [x_dev(up(x, d, NX)) for d in range(1, NX)]
    for peer in peers:
        pl.semaphore_signal(barrier, inc=1, device_id=peer, device_id_type=MESH)

    def base_of(c, k):
        return 512 * ((c + 2 * k) % NY) + 256 * k + LANES * (c // NY)

    for c in range(CH):
        for k in range(2):
            pltpu.make_async_copy(
                cot.at[:, pl.ds(base_of(c, k), LANES)],
                zbuf.at[c, z, :, pl.ds(LANES * k, LANES)], load_sem,
            ).start()
    pltpu.make_async_copy(hid_hbm, hid, hid_sem).start()
    for c in range(CH):
        for k in range(2):
            pltpu.make_async_copy(
                w_hbm.at[:, :, pl.ds(base_of(c, k), LANES)],
                wbuf.at[c, :, :, pl.ds(LANES * k, LANES)], w_sem,
            ).start()

    e_iota = lax.broadcasted_iota(jnp.int32, (64, LANES), 0)
    gates = gate_t[...].astype(F32)
    hit = jnp.zeros((64, LANES), F32)
    gate = jnp.zeros((64, LANES), F32)
    for k in range(8):
        eq = routes_t[k:k + 1, :] == e_iota
        hit = jnp.where(eq, 1.0, hit)
        gate = jnp.where(eq, gates[k:k + 1, :], gate)
    earlier = (
        lax.broadcasted_iota(jnp.int32, (LANES, LANES), 0)
        < lax.broadcasted_iota(jnp.int32, (LANES, LANES), 1)
    )
    rank = dot_nn(hit.astype(BF16), jnp.where(earlier, 1.0, 0.0).astype(BF16))
    table[z, 0:64, :] = jnp.where(hit > 0.5, rank, MISS).astype(BF16)
    table[z, 64:128, :] = gate.astype(BF16)
    pltpu.make_async_copy(zbuf.at[:, z], zbuf.at[:, z], load_sem).wait()
    pl.semaphore_wait(barrier, len(peers))

    lower, upper = pl.ds(0, 64), pl.ds(64, 64)

    def z_send(c, h):
        right, left = up(z, NZ - h, NZ), up(z, h, NZ)
        if h < 3:
            remote(zbuf.at[c, right], zbuf.at[c, right], zs_sem.at[0], z_recv.at[c, h], zr).start()
            remote(zbuf.at[c, left], zbuf.at[c, left], zs_sem.at[1], z_recv.at[c, h], zl).start()
        else:
            remote(zbuf.at[c, right, lower], zbuf.at[c, right, lower], zs_sem.at[0], z_recv.at[c, h], zr).start()
            remote(zbuf.at[c, left, upper], zbuf.at[c, left, upper], zs_sem.at[1], z_recv.at[c, h], zl).start()

    def z_wait(c, dist):
        wait_recv(zbuf.at[c, pl.ds(0, 2 if dist < 4 else 1)], z_recv.at[c, dist - 1])

    def z_relay(c, h):
        if h > 0:
            z_wait(c, h)
        z_send(c, h)

    def table_send(h):
        right, left = up(z, NZ - h, NZ), up(z, h, NZ)
        if h < 3:
            remote(table.at[right], table.at[right], tz_sem.at[0], tz_recv.at[h], zr).start()
            remote(table.at[left], table.at[left], tz_sem.at[1], tz_recv.at[h], zl).start()
        else:
            remote(table.at[right, lower], table.at[right, lower], tz_half.at[0], tz_recv.at[h], zr).start()
            remote(table.at[left, upper], table.at[left, upper], tz_half.at[1], tz_recv.at[h], zl).start()

    def table_rows(zs):
        block = table[zs].astype(F32)
        t_rows[zs] = block

    def table_wait(dist):
        wait_recv(table.at[pl.ds(0, 2 if dist < 4 else 1)], tz_recv.at[dist - 1])
        if dist < 4:
            table_send(dist)
            table_rows(up(z, NZ - dist, NZ))
        table_rows(up(z, dist, NZ))

    table_send(0)
    z_send(0, 0)
    z_send(1, 0)
    table_rows(z)

    r_iota = lax.broadcasted_iota(jnp.int32, (rows48, LANES), 0).astype(F32)

    def one_hot_pair(even_row, odd_row):
        return even_row == r_iota, odd_row + 24.0 == r_iota

    def build_sel(m):
        for dx in range(NX):
            xx = up(x, dx, NX)
            for j in range(2):
                row = pl.ds(16 * xx + 2 * z + j, 1)
                even, odd = one_hot_pair(t_rows[2 * m, row, :], t_rows[2 * m + 1, row, :])
                at = (dx * 2 + j) * rows48
                sel[m, at:at + rows48, 0:LANES] = jnp.where(even, 1.0, 0.0).astype(BF16)
                sel[m, at:at + rows48, LANES:2 * LANES] = jnp.where(odd, 1.0, 0.0).astype(BF16)

    def x_tables():
        for xx in range(NX):
            row = 16 * xx + 2 * z
            for zs in range(NZ):
                for j in range(2):
                    at = 2 * zs + j
                    x_rows[xx, at:at + 1, :] = t_rows[zs, pl.ds(row + j, 1), :]
                    x_rows[xx, 16 + at:17 + at, :] = t_rows[zs, pl.ds(64 + row + j, 1), :]
            x_out[xx] = x_rows[xx].astype(BF16)
        for d in range(1, NX):
            to = up(x, d, NX)
            remote(x_out.at[to], d_in.at[x], tx_sem, tx_recv, x_dev(to)).start()
        d_in[x] = x_out[x]

    step_sign = 2 * lax.rem(z, 2) - 1

    def pair_of(i):
        turn = jnp.where(i == 0, 0, jnp.where(i == 1, 4 + step_sign, jnp.where(i == 2, 4 - step_sign, 2)))
        return lax.rem(z // 2 + turn, 4)

    def step_of(s, t):
        if t < 0:
            s, t = s - 1, t + 8
        tail = s >= 1
        return (
            jnp.where(tail, 2 * s + t // 4, 2 * s + t % 2),
            jnp.where(tail, t % 4, t // 2),
        )

    def x_step(c, i):
        m = pair_of(i)
        tokens = zbuf[c, pl.ds(2 * m, 2)].reshape(2 * LANES, CW)
        rows = dot_nn(sel[m], tokens).astype(BF16)
        xsend[c, i] = rows[96:384].reshape(3, 2, rows48, CW)
        here = x * 4 + m
        remote(xsend.at[c, i, 1, 0], relay.at[c, i, 0], xs_sem.at[2], xrel_recv.at[c, i], xr).start()
        remote(xsend.at[c, i, 1, 1], relay.at[c, i, 1], xs_sem.at[3], xrel_recv.at[c, i], xl).start()
        remote(xsend.at[c, i, 0], rg.at[c, :, here], xs_sem.at[0], x_recv.at[c], xr).start()
        remote(xsend.at[c, i, 2], rg.at[c, :, here], xs_sem.at[1], x_recv.at[c], xl).start()
        rg[c, :, here] = rows[0:96].reshape(2, rows48, CW)

    def x_forward(c, i):
        m = pair_of(i)
        from_l, from_r = up(x, NX - 1, NX) * 4 + m, up(x, 1, NX) * 4 + m
        wait_recv(relay.at[c, i], xrel_recv.at[c, i])
        remote(relay.at[c, i, 0], rg.at[c, 0, from_l], xs_sem.at[4], x_recv.at[c], xr).start()
        remote(relay.at[c, i, 1], rg.at[c, 1, from_r], xs_sem.at[5], x_recv.at[c], xl).start()

    def x_wait(c):
        wait_recv(rg.at[c, :, pl.ds(0, 12)], x_recv.at[c])

    def pair_rows(p, j, row):
        xs, at = p // 4, 4 * lax.rem(p, 4) + j + row
        return d_tab[xs, pl.ds(at, 1), :], d_tab[xs, pl.ds(at + 2, 1), :]

    def slot_prob(p, j):
        even, odd = one_hot_pair(*pair_rows(p, j, 0))
        g_even, g_odd = pair_rows(p, j, 16)
        picked = jnp.where(even, g_even, 0.0) + jnp.where(odd, g_odd, 0.0)
        return jnp.sum(picked, axis=1, keepdims=True)

    def weigh():
        wait_recv(d_in.at[pl.ds(0, 3)], tx_recv)
        d_tab[...] = d_in[...].astype(F32)
        pltpu.make_async_copy(hid_hbm, hid, hid_sem).wait()

        def body(p, _):
            at = pl.ds(pl.multiple_of(p * rows48, 16), rows48)
            for j in range(2):
                rows = slot_prob(p, j) * hid[j, at, :].astype(F32)
                gh_buf[j, at, :] = rows.astype(BF16)
            return 0

        lax.fori_loop(0, 16, body, 0)
        for j in range(2):
            for q in range(6):
                cols = slice(LANES * q, LANES * (q + 1))
                weighted_t[j, cols, :] = gh_buf[j, :, cols].T

    def partial(c):
        for j in range(2):
            for q in range(3):
                fs = slice(256 * q, 256 * (q + 1))
                got = dot_nn(weighted_t[j, fs, :], rg[c, j].reshape(768, CW)).astype(BF16)
                for k in range(2):
                    part[c, k, j, fs, :] = got[:, LANES * k:LANES * (k + 1)]
            remote(part.at[c, 1 - core, j], part_in.at[c, j], p_send, p_recv.at[c], partner).start()

    def back(c):
        for j in range(2):
            for q in range(3):
                rs = slice(256 * q, 256 * (q + 1))
                acc[j, rs, :] += dot_nt(rg[c, j].reshape(768, CW)[rs], wbuf[c, j])

    def role(c):
        return up(y + NY, NY - lax.rem(c + 2 * core, NY), NY)

    def pair_add(c):
        half, at = c // NY, role(c)
        wait_recv(part_in.at[c], p_recv.at[c])
        for j in range(2):
            total = part[c, core, j].astype(F32) + part_in[c, j].astype(F32)
            part[c, core, j] = total.astype(BF16)
        mine = part.at[c, core]

        @pl.when(at == 2)
        def _():
            remote(mine.at[0], y_relay.at[half, 0], yr_send, yr_recv.at[half, 0], yr).start()
            remote(mine.at[1], y_relay.at[half, 1], yr_send, yr_recv.at[half, 1], yl).start()

        @pl.when(at == 3)
        def _():
            remote(mine.at[1], y_fin.at[half, 0, 1], yf_send, yf_recv.at[half], yr).start()

        @pl.when(at == 1)
        def _():
            remote(mine.at[0], y_fin.at[half, 1, 0], yf_send, yf_recv.at[half], yl).start()

    def relay_add(c):
        half, at = c // NY, role(c)
        for j, place, side, dev in ((0, 3, 0, yr), (1, 1, 1, yl)):
            @pl.when(at == place)
            def _(j=j, side=side, dev=dev):
                wait_recv(y_relay.at[half, j], yr_recv.at[half, j])
                total = part[c, core, j].astype(F32) + y_relay[half, j].astype(F32)
                part[c, core, j] = total.astype(BF16)
                remote(part.at[c, core, j], y_fin.at[half, side, j], yf_send, yf_recv.at[half], dev).start()

    def finish(c):
        half = c // NY

        @pl.when(role(c) == 0)
        def _():
            i0 = lax.broadcasted_iota(jnp.int32, (BLOCK, BLOCK), 0)
            i1 = lax.broadcasted_iota(jnp.int32, (BLOCK, BLOCK), 1)
            bits = i0 & i1
            bits = bits ^ (bits >> 4)
            bits = bits ^ (bits >> 2)
            bits = bits ^ (bits >> 1)
            sign = (2 * seed[pl.ds(4 * y + 2 * core + half, 1), :] - 1).astype(F32)
            turn = (jnp.where((bits & 1) == 1, -1.0, 1.0) * sign).astype(BF16)
            out_rows = pl.ds(pl.multiple_of(half * BLOCK, BLOCK), BLOCK)
            wait_recv(y_fin.at[half], yf_recv.at[half])
            for j in range(2):
                total = part[c, core, j].astype(F32) + y_fin[half, 0, j].astype(F32) + y_fin[half, 1, j].astype(F32)
                high = total.astype(BF16)
                low = (total - high.astype(F32)).astype(BF16)
                turned = (dot_nt(turn, high) + dot_nt(turn, low)) * (1.0 / math.sqrt(BLOCK))
                gw_buf[out_rows, 768 * j:768 * (j + 1)] = turned
            pltpu.make_async_copy(gw_buf.at[out_rows], gw_out.at[out_rows], out_sem.at[half]).start()

    acc[...] = jnp.zeros(acc.shape, F32)

    def double(s, _):
        first, more = s == 0, s > 0
        for t in range(8):
            q, h = t % 2, t // 2

            @pl.when(first)
            def _(q=q, h=h):
                z_wait(q, h + 1)
                if h < 3:
                    z_send(q, h + 1)
                if q == 0:
                    table_wait(h + 1)
                    build_sel(pair_of(h))

            if t in (0, 1, 2):
                @pl.when(more)
                def _(t=t):
                    if t == 0:
                        z_relay(2 * s + 1, 2)
                    else:
                        z_relay(2 * s + t - 1, 3)
            else:
                @pl.when(s < 3)
                def _(t=t):
                    z_relay(2 * s + 2 + (t - 3) % 2, (t - 3) // 2)

            c, i = step_of(s, t)
            if t in (3, 7):
                @pl.when(more)
                def _(c=c):
                    z_wait(c, 4)
            x_step(c, i)
            fc, fi = step_of(s, t - 3)
            if t < 3:
                @pl.when(more)
                def _(fc=fc, fi=fi):
                    x_forward(fc, fi)
            else:
                x_forward(fc, fi)

            at_one, later = s == 1, s > 1
            if t == 0:
                @pl.when(later)
                def _():
                    pair_add(2 * s - 3)
            if t == 2:
                @pl.when(at_one)
                def _():
                    weigh()

                @pl.when(later)
                def _():
                    x_wait(2 * s - 2)
                    partial(2 * s - 2)

                @pl.when(s == 2)
                def _():
                    relay_add(0)
            if t == 3:
                @pl.when(later)
                def _():
                    back(2 * s - 2)
                    relay_add(2 * s - 3)
            if t == 4:
                @pl.when(later)
                def _():
                    pair_add(2 * s - 2)
            if t == 5:
                @pl.when(at_one)
                def _():
                    pltpu.make_async_copy(wbuf, wbuf, w_sem).wait()
                    x_wait(0)
                    partial(0)
                    back(0)

                @pl.when(later)
                def _():
                    finish(jnp.where(s == 2, 0, 2))
            if t == 6:
                @pl.when(more)
                def _():
                    x_wait(2 * s - 1)
                    partial(2 * s - 1)
            if t == 7:
                @pl.when(first)
                def _():
                    x_tables()

                @pl.when(at_one)
                def _():
                    pair_add(0)

                @pl.when(more)
                def _():
                    back(2 * s - 1)

                @pl.when(later)
                def _():
                    relay_add(2 * s - 2)
                    finish(2 * s - 3)
        return 0

    lax.fori_loop(0, CH // 2, double, 0)

    x_forward(7, 1)
    x_forward(7, 2)
    pair_add(5)
    x_wait(6)
    partial(6)
    x_forward(7, 3)
    back(6)
    pair_add(6)
    relay_add(5)
    x_wait(7)
    partial(7)
    back(7)
    pair_add(7)
    relay_add(6)

    def outputs(p, _):
        at = pl.ds(pl.multiple_of(p * rows48, 16), rows48)
        xs, row = p // 4, 4 * lax.rem(p, 4)
        for j in range(2):
            rows = acc[j, at, :]
            gh_buf[j, at, :] = (slot_prob(p, j) * rows).astype(BF16)
            slot = jnp.sum(rows * hid[j, at, :].astype(F32), axis=1, keepdims=True)
            even, odd = one_hot_pair(*pair_rows(p, j, 0))
            r_tab[xs, pl.ds(row + j, 1), :] = jnp.sum(jnp.where(even, slot, 0.0), axis=0, keepdims=True)
            r_tab[xs, pl.ds(row + 2 + j, 1), :] = jnp.sum(jnp.where(odd, slot, 0.0), axis=0, keepdims=True)
        return 0

    for d in (2, 1, 3, 0):
        to = up(x, d, NX)
        lax.fori_loop(0, 4, lambda m, t, to=to: outputs(4 * to + m, t), 0)
        if d > 0:
            remote(r_tab.at[to], r_mid.at[x], rx_send, rx_recv, x_dev(to)).start()
        if d == 1:
            relay_add(7)
    r_mid[x] = r_tab[x]
    pltpu.make_async_copy(gh_buf, gh_out, hid_sem).start()
    finish(4)
    finish(5)
    wait_recv(r_mid.at[pl.ds(0, 3)], rx_recv)
    for zs in range(NZ):
        for xx in range(NX):
            r_out[zs, 2 * xx:2 * xx + 2, :] = r_mid[xx, 2 * zs:2 * zs + 2, :]
    for d in range(1, NZ):
        to = up(z, d, NZ)
        remote(r_out.at[to], r_end.at[z], rz_send, rz_recv, z_dev(to)).start()
    r_end[z] = r_out[z]
    finish(6)
    finish(7)
    wait_recv(r_end.at[pl.ds(0, 7)], rz_recv)
    grad_prob = jnp.zeros((8, LANES), F32)
    chosen = routes_t[...]
    for zz in range(NZ):
        for xx in range(NX):
            for j in range(2):
                e = 16 * xx + 2 * zz + j
                row = 2 * xx + j
                grad_prob = jnp.where(chosen == e, r_end[zz, row:row + 1, :], grad_prob)
    gp_out[...] = grad_prob

    wait_send(zbuf.at[pl.ds(0, 4), pl.ds(0, 7)], zs_sem.at[0])
    wait_send(zbuf.at[pl.ds(0, 4), pl.ds(0, 7)], zs_sem.at[1])
    for side in range(2):
        wait_send(table.at[pl.ds(0, 3)], tz_sem.at[side])
        wait_send(table.at[0, lower], tz_half.at[side])
        wait_send(xsend.at[:, :, 2 * side], xs_sem.at[side])
        wait_send(xsend.at[:, :, 1, side], xs_sem.at[2 + side])
        wait_send(relay.at[:, :, side], xs_sem.at[4 + side])
    wait_send(x_out.at[pl.ds(0, 3)], tx_sem)
    wait_send(r_tab.at[pl.ds(0, 3)], rx_send)
    wait_send(r_out.at[pl.ds(0, 7)], rz_send)
    wait_send(part.at[:, 0], p_send)
    wait_send(part.at[pl.ds(0, 2), 0], yr_send)
    wait_send(part.at[pl.ds(0, 4), 0], yf_send)
    pltpu.make_async_copy(gh_buf, gh_out, hid_sem).wait()
    for half in range(2):
        out_rows = pl.ds(BLOCK * half, BLOCK)
        pltpu.make_async_copy(gw_buf.at[out_rows], gw_out.at[out_rows], out_sem.at[half]).wait()


def shards(cotangent, gate_prob, routes, hidden, down_weight, sign_seed):
    tok, features = cotangent.shape
    _, pair, sources, cap, units = hidden.shape
    slots = sources * cap
    vm = pl.BlockSpec(memory_space=pltpu.VMEM)
    anyspec = pl.BlockSpec(memory_space=pl.ANY)
    dma = pltpu.SemaphoreType.DMA
    scratch = [
        pltpu.VMEM((CH, NZ, tok, CW), BF16),
        pltpu.VMEM((4, 384, 256), BF16),
        pltpu.VMEM((CH, 2, 16, 48, CW), BF16),
        pltpu.VMEM((CH, 4, 3, 2, 48, CW), BF16),
        pltpu.VMEM((CH, 4, 2, 48, CW), BF16),
        pltpu.VMEM((CH, 2, units, CW), BF16),
        pltpu.VMEM((2, slots, units), BF16),
        pltpu.VMEM((2, units, slots), BF16),
        pltpu.VMEM((2, slots, units), F32),
        pltpu.VMEM((2, slots, units), BF16),
        pltpu.VMEM((256, pair * units), F32),
        pltpu.VMEM((CH, 2, 2, units, LANES), BF16),
        pltpu.VMEM((CH, 2, units, LANES), BF16),
        pltpu.VMEM((2, 2, units, LANES), BF16),
        pltpu.VMEM((2, 2, 2, units, LANES), BF16),
        pltpu.VMEM((NZ, 128, LANES), BF16),
        pltpu.VMEM((NZ, 128, LANES), F32),
        pltpu.VMEM((NX, 32, LANES), F32),
        pltpu.VMEM((NX, 32, LANES), BF16),
        pltpu.VMEM((NX, 32, LANES), BF16),
        pltpu.VMEM((NX, 32, LANES), F32),
        pltpu.VMEM((NX, 16, LANES), F32),
        pltpu.VMEM((NX, 16, LANES), F32),
        pltpu.VMEM((NZ, 8, LANES), F32),
        pltpu.VMEM((NZ, 8, LANES), F32),
        dma, dma, dma, dma((2,)),
        dma((2,)), dma((CH, 4)),
        dma((2,)), dma((2,)), dma((4,)),
        dma((6,)), dma((CH,)), dma((CH, 4)),
        dma, dma,
        dma, dma((CH,)),
        dma, dma((2, 2)), dma, dma((2,)),
        dma, dma, dma, dma,
    ]
    grad_hidden, grad_prob, grad_weight = pl.pallas_call(
        kernel,
        out_shape=(
            jax.ShapeDtypeStruct((pair, slots, units), BF16),
            jax.ShapeDtypeStruct((8, tok), F32),
            jax.ShapeDtypeStruct((256, pair * units), F32),
        ),
        in_specs=[anyspec, anyspec, anyspec, vm, vm, vm],
        out_specs=(anyspec, vm, anyspec),
        scratch_shapes=scratch,
        compiler_params=pltpu.CompilerParams(
            collective_id=0, has_side_effects=True, vmem_limit_bytes=67043328
        ),
        name="routed_backward",
    )(
        cotangent,
        hidden.reshape(pair, slots, units),
        down_weight,
        routes.T,
        gate_prob.T,
        sign_seed.reshape(16, 128),
    )
    return (
        grad_hidden.reshape(hidden.shape),
        grad_prob.T,
        grad_weight.reshape(256, pair, units),
    )


def solution(mesh):
    in_specs = (
        P(("dp", "expert"), None),
        P(("dp", "expert"), None),
        P(("dp", "expert"), None),
        P("dp", "expert", None, None, None),
        P("expert", None, None),
        P(),
    )
    out_specs = (
        P("dp", "expert", None, None, None),
        P(("dp", "expert"), None),
        P("dp", "expert", None),
    )
    return jax.shard_map(shards, mesh=mesh, in_specs=in_specs, out_specs=out_specs, check_vma=False)
```
